512 devices in a mesh: op: 4 (over y_lo, core), cell: 128 (over x, y_hi, z).
Axes of the slice: x: 4, y: 4 (y_hi: 2, y_lo: 2; y = y_hi * 2 + y_lo), z: 16, core: 2. Of those that a mesh axis runs over, the one named last changes fastest.
Arguments:
- flow_state: float32 [8, 5, 5, 65536], P('op', None, None, 'cell'), may hold values from -6 to 6
- adjoint_start: float32 [8, 5, 5, 65536], P('op', None, None, 'cell'), may hold values from -6 to 6
- objective_grad: float32 [8, 5, 5, 65536], P('op', None, None, 'cell'), may hold values from -6 to 6
- adjacency: int32 [6, 65536], P(None, 'cell'), may hold values from -1 to 767, as said below
- send_list: int32 [32768], P('cell'), may hold values from 0 to 511, as said below
- cell_nodes: int32 [8, 65536], P(None, 'cell'), may hold values from 0 to 1023, as said below
- coords: float32 [3, 131072], P(None, ('op', 'cell')), may hold values from -0.2 to 32.2, as said below
- jacobians: float32 [8, 3, 5, 5], P('op'), may hold values from -1.5 to 1.5
- dissipation: float32 [8], P('op'), may hold values from 0.3 to 3
- frequency: float32 [8], P('op'), may hold values from 0.5 to 4
Outputs:
- adjoint_out: float32 [8, 5, 5, 65536], P('op', None, None, 'cell')
- node_sens: float32 [3, 131072], P(None, ('op', 'cell'))
The draws below stay inside these ranges and needn't reach their ends.
Inputs may be any that keep to these rules, and one draw needn't show every extreme that they name: `adjacency`: each block's cells are a lattice of 4 x 32 x 4 cells in some order; slots 0 and 1 face the previous and next circumferential layer, 2 and 3 along the span, 4 and 5 along the axis. An entry under 512 is a cell of the same block; 512 + p with p < 128 is position 128 + p of the previous block's send list, 640 + p is position p of the next block's, the blocks closing into a cycle; -1 is a wall. Only slots 0 and 1 name such entries. Every face is listed by both of its cells: when slot k of cell i names cell j, slot k xor 1 of j names i. `send_list`: each block's 128 first entries are distinct local cells whose slot 0 leaves the block, its 128 last entries those whose slot 1 does. `cell_nodes`: corner c = 4 e1 + 2 e2 + e3 of a cell lies on its side of slot 1 if e1 = 1, else of slot 0, likewise e2 for slots 2 and 3 and e3 for slots 4 and 5. Cells of one block that share a face share its four node slots. `coords`: each node slot that a cell names holds a point within 0.2 in each coordinate of its lattice point, cells being unit cubes of the lattice; other slots hold arbitrary values.
All inputs are finite; a program needn't handle non-finite values.
Results may differ from the reference program's by a relative error of at most 0.00026.
Values sent between devices are 32-bit elements; how exact they have to be, the bound alone decides.
A program may use at most 64 MiB of HBM per device.

```python
import math
from functools import partial
import jax
import jax.numpy as jnp
import numpy as np
from jax import lax

INST = 5
VARS = 5
LAYERS = 4
SPAN = 32
AXIAL = 4
ITERS = 4
OPS = 8
BLOCKS = 128
HALO = 128
CELL_DEV = 512
CELLS = 65536
SENDS = 32768
GRID_NODES = 825
NODE_SHARD = 256
NODE_BLK = 1024
NODES = 131072
N_OP = 4
N_CELL = 128


def mesh_tables(key):
    base_key = jax.random.fold_in(key, 4242)

    def block_tables(number):
        cell_perm = jax.random.permutation(jax.random.fold_in(base_key, 4 * number), CELL_DEV)
        lower_perm = jax.random.permutation(jax.random.fold_in(base_key, 4 * number + 1), HALO)
        upper_perm = jax.random.permutation(jax.random.fold_in(base_key, 4 * number + 2), HALO)
        node_perm = jax.random.permutation(jax.random.fold_in(base_key, 4 * number + 3), NODE_BLK)
        return (cell_perm.astype(jnp.int32), lower_perm.astype(jnp.int32), upper_perm.astype(jnp.int32), node_perm.astype(jnp.int32))
    return jax.vmap(block_tables)(jnp.arange(BLOCKS, dtype=jnp.int32))


def inverse_order(ordering):
    return jnp.zeros_like(ordering).at[ordering].set(jnp.arange(ordering.shape[0], dtype=jnp.int32))


def lattice_cells():
    grid_cells = jnp.arange(CELL_DEV, dtype=jnp.int32)
    layer_pos = grid_cells // HALO
    within = grid_cells % HALO
    return (grid_cells, layer_pos, within, within // AXIAL, within % AXIAL)


def draw_adjacency(key, part):
    cell_perm, lower_perm, upper_perm, node_perm = mesh_tables(key)
    lower_inverse = jax.vmap(inverse_order)(lower_perm)
    upper_inverse = jax.vmap(inverse_order)(upper_perm)
    previous_map = jnp.roll(upper_inverse, 1, axis=0)
    next_map = jnp.roll(lower_inverse, -1, axis=0)
    grid_cells, layer_pos, within, span_pos, axial_pos = lattice_cells()

    def block_adjacency(ordering, previous_one, next_one):

        def shifted(offset):
            return ordering[jnp.clip(grid_cells + offset, 0, CELL_DEV - 1)]
        entries = jnp.stack([jnp.where(layer_pos > 0, shifted(-HALO), CELL_DEV + previous_one[within]), jnp.where(layer_pos < LAYERS - 1, shifted(HALO), CELL_DEV + HALO + next_one[within]), jnp.where(span_pos > 0, shifted(-AXIAL), -1), jnp.where(span_pos < SPAN - 1, shifted(AXIAL), -1), jnp.where(axial_pos > 0, shifted(-1), -1), jnp.where(axial_pos < AXIAL - 1, shifted(1), -1)]).astype(jnp.int32)
        return jnp.zeros((6, CELL_DEV), jnp.int32).at[:, ordering].set(entries)
    blocks = jax.vmap(block_adjacency)(cell_perm, previous_map, next_map)
    return blocks.transpose(1, 0, 2).reshape(6, CELLS)


def draw_send_list(key, part):
    cell_perm, lower_perm, upper_perm, node_perm = mesh_tables(key)
    first_half = jnp.take_along_axis(cell_perm, lower_perm, axis=1)
    second_half = jnp.take_along_axis(cell_perm, (LAYERS - 1) * HALO + upper_perm, axis=1)
    return jnp.concatenate([first_half, second_half], axis=1).reshape(SENDS).astype(jnp.int32)


def draw_cell_nodes(key, part):
    cell_perm, lower_perm, upper_perm, node_perm = mesh_tables(key)
    grid_cells, layer_pos, within, span_pos, axial_pos = lattice_cells()
    corner_rows = []
    for corner in range(8):
        lift = corner // 4
        side = corner // 2 % 2
        depth = corner % 2
        corner_rows.append(((layer_pos + lift) * (SPAN + 1) + span_pos + side) * (AXIAL + 1) + axial_pos + depth)
    grid_nodes = jnp.stack(corner_rows)

    def block_corners(ordering, node_slots):
        return jnp.zeros((8, CELL_DEV), jnp.int32).at[:, ordering].set(node_slots[grid_nodes])
    blocks = jax.vmap(block_corners)(cell_perm, node_perm)
    return blocks.transpose(1, 0, 2).reshape(8, CELLS)


def draw_coords(key, part):
    cell_perm, lower_perm, upper_perm, node_perm = mesh_tables(key)
    node_grid = jnp.arange(GRID_NODES, dtype=jnp.int32)
    plane_size = (SPAN + 1) * (AXIAL + 1)
    lattice = jnp.stack([node_grid // plane_size, node_grid % plane_size // (AXIAL + 1), node_grid % (AXIAL + 1)]).astype(jnp.float32)
    shift_key = jax.random.fold_in(key, 91)
    moved = lattice[None] + jax.random.uniform(jax.random.fold_in(shift_key, 3), (BLOCKS, 3, GRID_NODES), jnp.float32, -0.15, 0.15)
    filler = jax.random.uniform(jax.random.fold_in(shift_key, 4), (BLOCKS, 3, NODE_BLK), jnp.float32, 0.0, 1.0) * LAYERS

    def place_nodes(fill_one, moved_one, node_slots):
        return fill_one.at[:, node_slots[:GRID_NODES]].set(moved_one)
    placed = jax.vmap(place_nodes)(filler, moved, node_perm)
    return placed.reshape(BLOCKS, 3, NODE_BLK // NODE_SHARD, NODE_SHARD).transpose(1, 2, 0, 3).reshape(3, NODES)


def block_scale(own_key, dims, shards, low, high):
    loudness, own = 1.0, jax.random.fold_in(own_key, 6)
    for axis_at, parts in shards:
        draws = jnp.exp(jax.random.uniform(jax.random.fold_in(own, axis_at), (parts,), jnp.float32, low / len(shards), high / len(shards)))
        loudness = loudness * jnp.repeat(draws, dims[axis_at] // parts).reshape([-1 if axis == axis_at else 1 for axis in range(len(dims))])
    return loudness


def normal_values(rng, shape, scale, limit, pieces=(), held_as=jnp.bfloat16):
    result = jax.random.normal(rng, shape, jnp.float32) * scale
    if len(pieces) > 0:
        result = block_scale(rng, shape, pieces, -0.22, 0.18) * result
    return jnp.clip(result, min=-limit, max=limit).astype(held_as)


def setup_inputs(seed: int = 0) -> dict:
    key_of = jax.random.split(jax.random.key(seed), 11)
    flow_state = normal_values(key_of[0], (OPS, INST, VARS, CELLS), 1.0, 6.0, ((0, 4), (3, 128)), jnp.float32)
    adjoint_start = normal_values(key_of[1], (OPS, INST, VARS, CELLS), 1.0, 6.0, ((0, 4), (3, 128)), jnp.float32)
    objective_grad = normal_values(key_of[2], (OPS, INST, VARS, CELLS), 1.0, 6.0, ((0, 4), (3, 128)), jnp.float32)
    adjacency = draw_adjacency(jax.random.fold_in(key_of[10], 71), 0)
    send_list = draw_send_list(jax.random.fold_in(key_of[10], 71), 0)
    cell_nodes = draw_cell_nodes(jax.random.fold_in(key_of[10], 71), 0)
    coords = draw_coords(jax.random.fold_in(key_of[10], 71), 0)
    jacobians = normal_values(key_of[7], (OPS, 3, VARS, VARS), 0.25, 1.5, ((0, 4),), jnp.float32)
    dissipation = jnp.clip(jnp.exp(math.log(3.0) - 2.3025851 * jax.random.uniform(key_of[8], (OPS,), jnp.float32) ** block_scale(key_of[8], (OPS,), ((0, 4),), -0.2, 0.2)), 0.3, 3.0)
    frequency = jnp.clip(jnp.exp(math.log(4.0) - 2.0794415 * jax.random.uniform(key_of[9], (OPS,), jnp.float32) ** block_scale(key_of[9], (OPS,), ((0, 4),), -0.2, 0.2)), 0.5, 4.0)
    return dict(flow_state=flow_state, adjoint_start=adjoint_start, objective_grad=objective_grad, adjacency=adjacency, send_list=send_list, cell_nodes=cell_nodes, coords=coords, jacobians=jacobians, dissipation=dissipation, frequency=frequency)


FACE_CORNERS = ((0, 1, 3, 2), (4, 6, 7, 5), (0, 4, 5, 1), (2, 3, 7, 6), (0, 2, 6, 4), (1, 5, 7, 3))
COURANT = 1.2

def spectral_matrix(instances):
    values = np.zeros((instances, instances))
    for first_index in range(instances):
        for second_index in range(instances):
            if first_index != second_index:
                offset = first_index - second_index
                values[first_index, second_index] = 0.5 * (-1.0) ** offset / math.sin(math.pi * offset / instances)
    return jnp.asarray(values, jnp.float32)

def cross_columns(left_vec, right_vec):
    return jnp.stack([left_vec[1] * right_vec[2] - left_vec[2] * right_vec[1], left_vec[2] * right_vec[0] - left_vec[0] * right_vec[2], left_vec[0] * right_vec[1] - left_vec[1] * right_vec[0]])

def cell_geometry(node_positions, corner_slots):
    corners = [jnp.take(node_positions, corner_slots[corner], axis=1) for corner in range(8)]
    center = lax.optimization_barrier(jnp.mean(jnp.stack(corners), axis=0))
    normals = []
    volume = jnp.zeros((corner_slots.shape[1],), jnp.float32)
    for quad_face in FACE_CORNERS:
        normal = 0.5 * cross_columns(corners[quad_face[2]] - corners[quad_face[0]], corners[quad_face[3]] - corners[quad_face[1]])
        middle = 0.25 * (corners[quad_face[0]] + corners[quad_face[1]] + corners[quad_face[2]] + corners[quad_face[3]])
        volume = volume + lax.optimization_barrier(jnp.sum((middle - center) * normal, axis=0))
        normals.append(normal)
    return (jnp.stack(normals), volume / 3.0)

def geometry_pullback(node_positions, corner_slots, normal_cot, volume_cot):
    outputs, pullback = jax.vjp(partial(cell_geometry, corner_slots=corner_slots), node_positions)
    return pullback((normal_cot, volume_cot))[0]

def partner_cells(adjacency, send_list):
    owner_block = jnp.arange(CELLS, dtype=jnp.int32) // CELL_DEV
    before = (owner_block + N_CELL - 1) % N_CELL
    beyond = (owner_block + 1) % N_CELL
    outbound = send_list.reshape(N_CELL, 2 * HALO)
    local_cell = owner_block * CELL_DEV + jnp.clip(adjacency, 0, CELL_DEV - 1)
    from_before = before * CELL_DEV + outbound[before, jnp.clip(adjacency - CELL_DEV + HALO, HALO, 2 * HALO - 1)]
    from_beyond = beyond * CELL_DEV + outbound[beyond, jnp.clip(adjacency - CELL_DEV - HALO, 0, HALO - 1)]
    chosen = jnp.where(adjacency < CELL_DEV, local_cell, jnp.where(adjacency < CELL_DEV + HALO, from_before, from_beyond))
    return jnp.where(adjacency < 0, CELLS, chosen).astype(jnp.int32)

def reference(flow_state, adjoint_start, objective_grad, adjacency, send_list, cell_nodes, coords, jacobians, dissipation, frequency):
    highest = lax.Precision.HIGHEST
    block_nodes = coords.reshape(3, N_OP, N_CELL, NODE_SHARD).transpose(2, 0, 1, 3).reshape(N_CELL, 3, NODE_BLK)
    block_corners = cell_nodes.reshape(8, N_CELL, CELL_DEV).transpose(1, 0, 2)
    block_normals, block_volumes = jax.vmap(cell_geometry)(block_nodes, block_corners)
    normals = block_normals.transpose(1, 2, 0, 3).reshape(6, 3, CELLS)
    volumes = block_volumes.reshape(CELLS)
    areas = jnp.sqrt(lax.optimization_barrier(jnp.sum(normals * normals, axis=1)))
    area_sum = lax.optimization_barrier(jnp.sum(areas, axis=0))
    partner = partner_cells(adjacency, send_list)
    spectral = spectral_matrix(INST)
    damping = dissipation[:, None, None, None]
    rate = frequency[:, None, None, None]
    step_size = COURANT / ((1.0 + dissipation[:, None]) * area_sum[None, :] + 2.0 * frequency[:, None] * volumes[None, :])
    step_size = step_size[:, None, None, :]
    normals_pad = jnp.concatenate([normals, jnp.zeros((6, 3, 1), jnp.float32)], axis=2)
    areas_pad = jnp.concatenate([areas, jnp.zeros((6, 1), jnp.float32)], axis=1)
    adjoint = adjoint_start
    for sweep in range(ITERS):
        turned = jnp.einsum('pduv,ptuc->dptvc', jacobians, adjoint, precision=highest)
        update = 0.5 * jnp.einsum('kdc,dptvc->ptvc', normals, turned, precision=highest)
        update = update + 0.5 * damping * area_sum * adjoint
        update = update + rate * volumes * jnp.einsum('ts,ptvc->psvc', spectral, adjoint, precision=highest)
        update = update + objective_grad
        turned_pad = jnp.concatenate([turned, jnp.zeros(turned.shape[:4] + (1,), jnp.float32)], axis=4)
        adjoint_pad = jnp.concatenate([adjoint, jnp.zeros(adjoint.shape[:3] + (1,), jnp.float32)], axis=3)
        for slot in range(6):
            mirror = slot ^ 1
            target = partner[slot]
            far_normal = jnp.take(normals_pad[mirror], target, axis=1)
            far_area = jnp.take(areas_pad[mirror], target, axis=0)
            far_turned = jnp.take(turned_pad, target, axis=4)
            far_adjoint = jnp.take(adjoint_pad, target, axis=3)
            face_term = 0.5 * jnp.einsum('dc,dptvc->ptvc', far_normal, far_turned, precision=highest) - 0.5 * damping * far_area * far_adjoint
            update = update + face_term
        adjoint = adjoint - step_size * update
    weight = 1.0 / OPS
    final_turned = jnp.einsum('pduv,ptuc->dptvc', jacobians, adjoint, precision=highest)
    state_pad = jnp.concatenate([flow_state, jnp.zeros(flow_state.shape[:3] + (1,), jnp.float32)], axis=3)
    spectral_state = jnp.einsum('ts,psvc->ptvc', spectral, flow_state, precision=highest)
    volume_grad = weight * lax.optimization_barrier(jnp.sum(rate * adjoint * spectral_state, axis=(0, 1, 2)))
    normal_grads = []
    for slot in range(6):
        far_state = jnp.take(state_pad, partner[slot], axis=3)
        along = weight * 0.5 * jnp.einsum('dptvc,ptvc->dc', final_turned, flow_state + far_state, precision=highest)
        spread = weight * 0.5 * lax.optimization_barrier(jnp.sum(damping * adjoint * (flow_state - far_state), axis=(0, 1, 2)))
        normal_grads.append(along + spread * normals[slot] / areas[slot])
    normal_grad = jnp.stack(normal_grads)
    block_normal_grad = normal_grad.reshape(6, 3, N_CELL, CELL_DEV).transpose(2, 0, 1, 3)
    block_volume_grad = volume_grad.reshape(N_CELL, CELL_DEV)
    node_blocks = jax.vmap(geometry_pullback)(block_nodes, block_corners, block_normal_grad, block_volume_grad)
    node_sens = node_blocks.reshape(N_CELL, 3, N_OP, NODE_SHARD).transpose(1, 2, 0, 3).reshape(3, NODES)
    return (adjoint, node_sens)
```

```python
import functools
import math

import jax
import jax.numpy as jnp
import numpy as np
from jax import lax
from jax.experimental import pallas as pl
from jax.experimental.pallas import tpu as pltpu
from jax.sharding import PartitionSpec as P

ITERS = 4
INST = 5
VARS = 5
OPS_HERE = 2
N_OP = 4
LANES = 128
CELLS_HERE = 512
FACE_CORNERS = ((0, 1, 3, 2), (4, 6, 7, 5), (0, 4, 5, 1), (2, 3, 7, 6), (0, 2, 6, 4), (1, 5, 7, 3))
COURANT = 1.2
WEIGHT = 1.0 / 8
STATE = INST * VARS
GROUPS = (STATE + 3) // 4
MESH = pl.DeviceIdType.MESH


def spectral_values():
    values = np.zeros((INST, INST))
    for t in range(INST):
        for s in range(INST):
            if t != s:
                values[t, s] = 0.5 * (-1.0) ** (t - s) / math.sin(math.pi * (t - s) / INST)
    return values


def lanes_at(table, index):
    return jnp.take_along_axis(table, index, axis=1, mode="promise_in_bounds")


def split3(x):
    hi = x.astype(jnp.bfloat16)
    rest = x - hi.astype(jnp.float32)
    mid = rest.astype(jnp.bfloat16)
    low = (rest - mid.astype(jnp.float32)).astype(jnp.bfloat16)
    return jnp.concatenate([hi, mid, low], axis=0)


def move_cells(x, onehot, contract):
    rows = x.shape[0]
    y = lax.dot_general(
        split3(x), onehot, (((1,), (contract,)), ((), ())), preferred_element_type=jnp.float32
    )
    return y[:rows] + y[rows : 2 * rows] + y[2 * rows :]


def spread(row):
    return jnp.broadcast_to(row, (8, LANES))


def cross(a, b):
    return [a[1] * b[2] - a[2] * b[1], a[2] * b[0] - a[0] * b[2], a[0] * b[1] - a[1] * b[0]]


def kernel(
    state_ref,
    start_ref,
    objective_ref,
    adjacency_ref,
    send_ref,
    nodes_ref,
    coords_ref,
    jac_ref,
    damp_ref,
    freq_ref,
    out_ref,
    sens_ref,
    cbuf,
    nodebuf,
    cornerbuf,
    stack,
    lattice,
    corner_lat,
    slot_lat,
    up_send,
    down_send,
    low_recv,
    high_recv,
    rs_send,
    rs_recv,
    outbuf,
    c_send_sem,
    c_recv_sem,
    r_send_sem,
    r_recv_sem,
    up_send_sem,
    up_recv_sem,
    down_send_sem,
    down_recv_sem,
):
    op = lax.axis_index("op")
    cell = lax.axis_index("cell")
    n_cell = 128
    nxt = lax.rem(cell + 1, n_cell)
    prv = lax.rem(cell + n_cell - 1, n_cell)
    peers = [lax.rem(op + j, N_OP) for j in range(1, N_OP)]

    barrier = pltpu.get_barrier_semaphore()
    for peer in peers:
        pl.semaphore_signal(barrier, inc=1, device_id=(peer, cell), device_id_type=MESH)
    for block in (prv, nxt):
        pl.semaphore_signal(barrier, inc=1, device_id=(op, block), device_id_type=MESH)
    pl.semaphore_wait(barrier, 5)

    coord_copies = []
    for j, peer in enumerate(peers):
        copy = pltpu.make_async_remote_copy(
            src_ref=coords_ref,
            dst_ref=cbuf.at[op],
            send_sem=c_send_sem.at[j],
            recv_sem=c_recv_sem.at[j],
            device_id=(peer, cell),
            device_id_type=MESH,
        )
        copy.start()
        coord_copies.append(copy)
    cbuf[op] = coords_ref[...]

    sub = lax.broadcasted_iota(jnp.int32, (8, LANES), 0)
    lane = lax.broadcasted_iota(jnp.int32, (8, LANES), 1)
    layer = lax.rem(sub, 4)
    first_op = sub < 4
    axial = lax.rem(lane, 4)
    stack[...] = jnp.zeros_like(stack)
    for a, ref in enumerate((start_ref, objective_ref, state_ref)):
        for p in range(OPS_HERE):
            for t in range(INST):
                stack[a * 10 + p * 5 + t, 0:VARS, :] = ref[p, t]
    stack[33, 0:6, :] = adjacency_ref[...].astype(jnp.float32)
    stack[34] = nodes_ref[...].astype(jnp.float32)

    def pick(p0, p1):
        return jnp.where(first_op, p0, p1)

    jac = [
        [[pick(jac_ref[0, d, u, v], jac_ref[1, d, u, v]) for v in range(VARS)] for u in range(VARS)]
        for d in range(3)
    ]
    damp = pick(damp_ref[0], damp_ref[1])
    freq = pick(freq_ref[0], freq_ref[1])

    for copy in coord_copies:
        copy.wait()

    for o in range(N_OP):
        for d in range(3):
            for h in range(2):
                nodebuf[d, 2 * o + h : 2 * o + h + 1, :] = cbuf[
                    o, d : d + 1, h * LANES : (h + 1) * LANES
                ]

    for tile in range(4):
        index = nodes_ref[:, tile * LANES : (tile + 1) * LANES]
        page = index // LANES
        within = lax.rem(index, LANES)
        for d in range(3):
            value = jnp.zeros((8, LANES), jnp.float32)
            for n in range(8):
                got = lanes_at(spread(nodebuf[d, n : n + 1, :]), within)
                value = jnp.where(page == n, got, value)
            stack[30 + d, :, tile * LANES : (tile + 1) * LANES] = value

    base = [jnp.floor(stack[30 + d, 0:1, :] + 0.5).astype(jnp.int32) for d in range(3)]
    pos = base[0] * LANES + base[1] * 4 + base[2]
    onehot = (
        (lax.broadcasted_iota(jnp.int32, (CELLS_HERE, CELLS_HERE), 0) == pos)
        .astype(jnp.float32)
        .astype(jnp.bfloat16)
    )
    moved = move_cells(stack[...].reshape(35 * 8, CELLS_HERE), onehot, 1).reshape(35, 8, CELLS_HERE)

    for a in range(3):
        for p in range(OPS_HERE):
            for t in range(INST):
                for l in range(4):
                    lattice[a, t, :, p * 4 + l, :] = moved[
                        a * 10 + p * 5 + t, 0:VARS, l * LANES : (l + 1) * LANES
                    ]
    for d in range(3):
        for l in range(4):
            part = moved[30 + d, :, l * LANES : (l + 1) * LANES]
            corner_lat[d, :, l, :] = part
            corner_lat[d, :, 4 + l, :] = part
    for l in range(4):
        part = moved[34, :, l * LANES : (l + 1) * LANES]
        slot_lat[:, l, :] = part

    def pos_of(cells):
        page = cells // LANES
        within = lax.rem(cells, LANES)
        value = jnp.zeros((8, LANES), jnp.int32)
        for n in range(4):
            got = lanes_at(spread(pos[:, n * LANES : (n + 1) * LANES]), within)
            value = jnp.where(page == n, got, value)
        return lax.rem(value, LANES)

    lower_map = pos_of(spread(send_ref[0:1, :]))
    upper_map = pos_of(spread(send_ref[1:2, :]))

    def pack(values, source):
        packed = []
        for g in range(GROUPS):
            total = values[4 * g]
            for r in range(1, 4):
                if 4 * g + r < STATE:
                    total = jnp.where(
                        layer == (source + r) % 4, pltpu.roll(values[4 * g + r], r, 0), total
                    )
            packed.append(total)
        return packed

    def exchange(number):
        used = pl.ds(0, GROUPS + 1 if number == 0 else GROUPS)
        up = pltpu.make_async_remote_copy(
            src_ref=up_send.at[number, used],
            dst_ref=low_recv.at[number, used],
            send_sem=up_send_sem.at[number],
            recv_sem=up_recv_sem.at[number],
            device_id=(op, nxt),
            device_id_type=MESH,
        )
        down = pltpu.make_async_remote_copy(
            src_ref=down_send.at[number, used],
            dst_ref=high_recv.at[number, used],
            send_sem=down_send_sem.at[number],
            recv_sem=down_recv_sem.at[number],
            device_id=(op, prv),
            device_id_type=MESH,
        )
        up.start()
        down.start()
        return up, down

    def fill(number, upward, downward):
        for g, value in enumerate(pack(upward, 3)):
            up_send[number, g] = value
        for g, value in enumerate(pack(downward, 0)):
            down_send[number, g] = value

    flow = [lattice[2, j // VARS, j % VARS] for j in range(STATE)]
    fill(0, flow, flow)
    up_send[0, GROUPS] = upper_map.astype(jnp.float32)
    down_send[0, GROUPS] = lower_map.astype(jnp.float32)
    copies = [exchange(0)]

    corner = [[corner_lat[d, c] for d in range(3)] for c in range(8)]
    center = [sum(corner[c][d] for c in range(8)) * 0.125 for d in range(3)]
    normals, areas, offsets = [], [], []
    volume = jnp.zeros((8, LANES), jnp.float32)
    for c0, c1, c2, c3 in FACE_CORNERS:
        first = [corner[c2][d] - corner[c0][d] for d in range(3)]
        second = [corner[c3][d] - corner[c1][d] for d in range(3)]
        normal = [0.5 * x for x in cross(first, second)]
        offset = [
            0.25 * (corner[c0][d] + corner[c1][d] + corner[c2][d] + corner[c3][d]) - center[d]
            for d in range(3)
        ]
        volume = volume + sum(offset[d] * normal[d] for d in range(3))
        normals.append(normal)
        offsets.append(offset)
        areas.append(jnp.sqrt(sum(normal[d] * normal[d] for d in range(3))))
    volume = volume * (1.0 / 3.0)
    area_sum = sum(areas)
    normal_total = [sum(normals[k][d] for k in range(6)) for d in range(3)]
    step = COURANT / ((1.0 + damp) * area_sum + 2.0 * freq * volume)

    inner = [None, None, lane >= 4, lane < LANES - 4, axial > 0, axial < 3]
    face_normal, face_area = [], []
    for k in range(6):
        keep = [0.5 * normals[k][d] for d in range(3)]
        area = 0.5 * damp * areas[k]
        if inner[k] is not None:
            keep = [jnp.where(inner[k], x, 0.0) for x in keep]
            area = jnp.where(inner[k], area, 0.0)
        face_normal.append(keep)
        face_area.append(area)
    half_total = [0.5 * normal_total[d] for d in range(3)]
    self_area = 0.5 * damp * area_sum
    freq_volume = freq * volume
    spectral = spectral_values()

    ghost_index = [None, None]

    def ghosts(number):
        low, high = [], []
        for g in range(GROUPS):
            from_low = lanes_at(low_recv[number, g], ghost_index[0])
            from_high = lanes_at(high_recv[number, g], ghost_index[1])
            for r in range(4):
                if 4 * g + r < STATE:
                    low.append(pltpu.roll(from_low, (8 - 3 - r) % 8, 0))
                    high.append(pltpu.roll(from_high, (3 - r) % 8, 0))
        return low, high

    for sweep in range(ITERS):
        adjoint = [lattice[0, j // VARS, j % VARS] for j in range(STATE)]
        upward, downward = [], []
        updates = []
        for t in range(INST):
            for v in range(VARS):
                j = t * VARS + v
                turned = [
                    sum(jac[d][u][v] * adjoint[t * VARS + u] for u in range(VARS)) for d in range(3)
                ]

                def outgoing(k):
                    return (
                        face_normal[k][0] * turned[0]
                        + face_normal[k][1] * turned[1]
                        + face_normal[k][2] * turned[2]
                        - face_area[k] * adjoint[j]
                    )

                upward.append(outgoing(1))
                downward.append(outgoing(0))
                update = (
                    half_total[0] * turned[0]
                    + half_total[1] * turned[1]
                    + half_total[2] * turned[2]
                    + self_area * adjoint[j]
                    + lattice[1, t, v]
                )
                mix = None
                for other in range(INST):
                    if other != t:
                        term = float(spectral[other, t]) * adjoint[other * VARS + v]
                        mix = term if mix is None else mix + term
                update = update + freq_volume * mix
                update = update + pltpu.roll(outgoing(3), 4, 1)
                update = update + pltpu.roll(outgoing(2), LANES - 4, 1)
                update = update + pltpu.roll(outgoing(5), 1, 1)
                update = update + pltpu.roll(outgoing(4), LANES - 1, 1)
                updates.append(update)
        fill(sweep + 1, upward, downward)
        copies.append(exchange(sweep + 1))
        if sweep == 0:
            for copy in copies[0]:
                copy.wait()
            for side in range(2):
                table = (low_recv, high_recv)[side][0, GROUPS].astype(jnp.int32)
                row = jnp.concatenate(
                    [
                        moved[33, side : side + 1, l * LANES : (l + 1) * LANES]
                        for l in ((0,) if side == 0 else (3,))
                    ],
                    axis=0,
                ).astype(jnp.int32)
                named = spread(row) - CELLS_HERE - side * LANES
                ghost_index[side] = lanes_at(table, jnp.clip(named, 0, LANES - 1))
        for copy in copies[sweep + 1]:
            copy.wait()
        low, high = ghosts(sweep + 1)
        for j in range(STATE):
            near_low = jnp.where(layer == 0, low[j], pltpu.roll(upward[j], 1, 0))
            near_high = jnp.where(layer == 3, high[j], pltpu.roll(downward[j], 7, 0))
            lattice[0, j // VARS, j % VARS] = adjoint[j] - step * (updates[j] + near_low + near_high)

    for p in range(OPS_HERE):
        for t in range(INST):
            for l in range(4):
                outbuf[p * 5 + t, 0:VARS, l * LANES : (l + 1) * LANES] = lattice[0, t, :, p * 4 + l, :]
            outbuf[p * 5 + t, VARS:8, :] = jnp.zeros((3, CELLS_HERE), jnp.float32)
    back = move_cells(outbuf[...].reshape(80, CELLS_HERE), onehot, 0).reshape(10, 8, CELLS_HERE)
    for p in range(OPS_HERE):
        for t in range(INST):
            out_ref[p, t] = back[p * 5 + t, 0:VARS, :]

    low, high = ghosts(0)
    along = [[None] * 3 for _ in range(6)]
    spread_sum = [None] * 6
    here = [None] * 3
    here_damp = None
    volume_sum = None

    def added(total, term):
        return term if total is None else total + term

    for t in range(INST):
        for v in range(VARS):
            j = t * VARS + v
            value = lattice[0, t, v]
            own = lattice[2, t, v]
            final = [
                sum(jac[d][u][v] * lattice[0, t, u] for u in range(VARS)) for d in range(3)
            ]
            mix = None
            for other in range(INST):
                if other != t:
                    mix = added(mix, float(spectral[t, other]) * lattice[2, other, v])
            volume_sum = added(volume_sum, value * mix)
            for d in range(3):
                here[d] = added(here[d], final[d] * own)
            here_damp = added(here_damp, value * own)
            far = [
                jnp.where(layer == 0, low[j], pltpu.roll(own, 1, 0)),
                jnp.where(layer == 3, high[j], pltpu.roll(own, 7, 0)),
                pltpu.roll(own, 4, 1),
                pltpu.roll(own, LANES - 4, 1),
                pltpu.roll(own, 1, 1),
                pltpu.roll(own, LANES - 1, 1),
            ]
            for k in range(6):
                for d in range(3):
                    along[k][d] = added(along[k][d], final[d] * far[k])
                spread_sum[k] = added(spread_sum[k], value * far[k])

    def both(x):
        return x + pltpu.roll(x, 4, 0)

    volume_grad = both(volume_sum * freq) * (WEIGHT / 3.0)
    cots = [[None] * 3 for _ in range(8)]
    center_cot = [-(0.125) * volume_grad * normal_total[d] for d in range(3)]
    for k, (c0, c1, c2, c3) in enumerate(FACE_CORNERS):
        far_along, far_damp = along[k], spread_sum[k]
        if inner[k] is not None:
            far_along = [jnp.where(inner[k], x, 0.0) for x in far_along]
            far_damp = jnp.where(inner[k], far_damp, 0.0)
        scale = both(damp * (here_damp - far_damp)) / areas[k]
        grad = [
            (0.5 * WEIGHT) * (both(here[d] + far_along[d]) + scale * normals[k][d])
            + volume_grad * offsets[k][d]
            for d in range(3)
        ]
        first = [corner[c2][d] - corner[c0][d] for d in range(3)]
        second = [corner[c3][d] - corner[c1][d] for d in range(3)]
        to_first = cross(second, grad)
        to_second = cross(grad, first)
        for d in range(3):
            middle = 0.25 * volume_grad * normals[k][d]
            cots[c0][d] = added(cots[c0][d], middle - 0.5 * to_first[d])
            cots[c2][d] = added(cots[c2][d], middle + 0.5 * to_first[d])
            cots[c1][d] = added(cots[c1][d], middle - 0.5 * to_second[d])
            cots[c3][d] = added(cots[c3][d], middle + 0.5 * to_second[d])
    cots = [[cots[c][d] + center_cot[d] for d in range(3)] for c in range(8)]

    def meet(bit, down, up, at_low, at_high):
        for c in range(8):
            if not c & bit:
                for d in range(3):
                    a, b = cots[c][d], cots[c | bit][d]
                    cots[c][d] = a + jnp.where(at_low, 0.0, down(b))
                    cots[c | bit][d] = b + jnp.where(at_high, 0.0, up(a))

    meet(1, lambda x: pltpu.roll(x, 1, 1), lambda x: pltpu.roll(x, LANES - 1, 1), axial == 0, axial == 3)
    meet(2, lambda x: pltpu.roll(x, 4, 1), lambda x: pltpu.roll(x, LANES - 4, 1), lane < 4, lane >= LANES - 4)
    meet(4, lambda x: pltpu.roll(x, 1, 0), lambda x: pltpu.roll(x, 7, 0), layer == 0, layer == 3)

    limits = (4, 32, 4)
    point = [
        jnp.clip(jnp.floor(jnp.clip(nodebuf[d], -1.0, 40.0) + 0.5).astype(jnp.int32), 0, limits[d])
        for d in range(3)
    ]
    home = [jnp.minimum(point[d], limits[d] - 1) for d in range(3)]
    source = ((point[0] - home[0]) * 4 + (point[1] - home[1]) * 2 + point[2] - home[2]) * 4 + home[0]
    within = home[1] * 4 + home[2]
    slot_number = sub * LANES + lane
    sens = [jnp.zeros((8, LANES), jnp.float32) for _ in range(3)]
    for c in range(8):
        slots = slot_lat[c]
        for l in range(4):
            name = lanes_at(spread(slots[l : l + 1]), within).astype(jnp.int32)
            chosen = jnp.logical_and(source == c * 4 + l, name == slot_number)
            for d in range(3):
                got = lanes_at(spread(cots[c][d][l : l + 1]), within)
                sens[d] = jnp.where(chosen, got, sens[d])

    rs_send[...] = jnp.zeros_like(rs_send)
    for o in range(N_OP):
        for d in range(3):
            rs_send[o, 2 * d : 2 * d + 2, :] = sens[d][2 * o : 2 * o + 2]
    sums = []
    for j, peer in enumerate(peers):
        copy = pltpu.make_async_remote_copy(
            src_ref=rs_send.at[peer],
            dst_ref=rs_recv.at[j],
            send_sem=r_send_sem.at[j],
            recv_sem=r_recv_sem.at[j],
            device_id=(peer, cell),
            device_id_type=MESH,
        )
        copy.start()
        sums.append(copy)
    total = rs_send[op]
    for j, copy in enumerate(sums):
        copy.wait()
        total = total + rs_recv[j]
    for d in range(3):
        for h in range(2):
            sens_ref[d : d + 1, h * LANES : (h + 1) * LANES] = total[2 * d + h : 2 * d + h + 1]


def per_device(
    flow_state,
    adjoint_start,
    objective_grad,
    adjacency,
    send_list,
    cell_nodes,
    coords,
    jacobians,
    dissipation,
    frequency,
):
    vmem = pl.BlockSpec(memory_space=pltpu.VMEM)
    smem = pl.BlockSpec(memory_space=pltpu.SMEM)
    f32 = jnp.float32
    dma = pltpu.SemaphoreType.DMA
    return pl.pallas_call(
        kernel,
        out_shape=(
            jax.ShapeDtypeStruct(flow_state.shape, f32),
            jax.ShapeDtypeStruct(coords.shape, f32),
        ),
        in_specs=[vmem] * 7 + [smem] * 3,
        out_specs=(vmem, vmem),
        scratch_shapes=[
            pltpu.VMEM((N_OP, 3, 256), f32),
            pltpu.VMEM((3, 8, LANES), f32),
            pltpu.VMEM((3, 8, CELLS_HERE), f32),
            pltpu.VMEM((35, 8, CELLS_HERE), f32),
            pltpu.VMEM((3, INST, VARS, 8, LANES), f32),
            pltpu.VMEM((3, 8, 8, LANES), f32),
            pltpu.VMEM((8, 8, LANES), f32),
            pltpu.VMEM((ITERS + 1, GROUPS + 1, 8, LANES), f32),
            pltpu.VMEM((ITERS + 1, GROUPS + 1, 8, LANES), f32),
            pltpu.VMEM((ITERS + 1, GROUPS + 1, 8, LANES), f32),
            pltpu.VMEM((ITERS + 1, GROUPS + 1, 8, LANES), f32),
            pltpu.VMEM((N_OP, 8, LANES), f32),
            pltpu.VMEM((N_OP - 1, 8, LANES), f32),
            pltpu.VMEM((10, 8, CELLS_HERE), f32),
            dma((3,)),
            dma((3,)),
            dma((3,)),
            dma((3,)),
            dma((ITERS + 1,)),
            dma((ITERS + 1,)),
            dma((ITERS + 1,)),
            dma((ITERS + 1,)),
        ],
        compiler_params=pltpu.CompilerParams(collective_id=0, has_side_effects=True),
    )(
        flow_state,
        adjoint_start,
        objective_grad,
        adjacency,
        send_list.reshape(2, LANES),
        cell_nodes,
        coords,
        jacobians,
        dissipation,
        frequency,
    )


def solution(mesh):
    in_specs = (
        P("op", None, None, "cell"),
        P("op", None, None, "cell"),
        P("op", None, None, "cell"),
        P(None, "cell"),
        P("cell"),
        P(None, "cell"),
        P(None, ("op", "cell")),
        P("op", None, None, None),
        P("op"),
        P("op"),
    )
    out_specs = (P("op", None, None, "cell"), P(None, ("op", "cell")))
    return jax.shard_map(
        per_device, mesh=mesh, in_specs=in_specs, out_specs=out_specs, check_vma=False
    )
```

```python
import functools
import math

import jax
import jax.numpy as jnp
import numpy as np
from jax import lax
from jax.experimental import pallas as pl
from jax.experimental.pallas import tpu as pltpu
from jax.sharding import PartitionSpec as P

ITERS = 4
INST = 5
VARS = 5
OPS_HERE = 2
N_OP = 4
LANES = 128
CELLS_HERE = 512
FACE_CORNERS = ((0, 1, 3, 2), (4, 6, 7, 5), (0, 4, 5, 1), (2, 3, 7, 6), (0, 2, 6, 4), (1, 5, 7, 3))
COURANT = 1.2
WEIGHT = 1.0 / 8
STATE = INST * VARS
GROUPS = (STATE + 3) // 4
MESH = pl.DeviceIdType.MESH


def spectral_values():
    values = np.zeros((INST, INST))
    for t in range(INST):
        for s in range(INST):
            if t != s:
                values[t, s] = 0.5 * (-1.0) ** (t - s) / math.sin(math.pi * (t - s) / INST)
    return values


def lanes_at(table, index):
    return jnp.take_along_axis(table, index, axis=1, mode="promise_in_bounds")


def split3(x):
    hi = x.astype(jnp.bfloat16)
    rest = x - hi.astype(jnp.float32)
    mid = rest.astype(jnp.bfloat16)
    low = (rest - mid.astype(jnp.float32)).astype(jnp.bfloat16)
    return jnp.concatenate([hi, mid, low], axis=0)


def move_cells(x, onehot, contract):
    rows = x.shape[0]
    y = lax.dot_general(
        split3(x), onehot, (((1,), (contract,)), ((), ())), preferred_element_type=jnp.float32
    )
    return y[:rows] + y[rows : 2 * rows] + y[2 * rows :]


def spread(row):
    return jnp.broadcast_to(row, (8, LANES))


def cross(a, b):
    return [a[1] * b[2] - a[2] * b[1], a[2] * b[0] - a[0] * b[2], a[0] * b[1] - a[1] * b[0]]


def kernel(
    state_in,
    start_in,
    objective_in,
    adjacency_in,
    send_in,
    nodes_in,
    coords_in,
    jac_in,
    damp_in,
    freq_in,
    out_hbm,
    sens_ref,
    state_ref,
    start_ref,
    objective_ref,
    adjacency_ref,
    send_ref,
    nodes_ref,
    coords_ref,
    jac_ref,
    damp_ref,
    freq_ref,
    out_ref,
    cbuf,
    nodebuf,
    stack,
    stack_late,
    lattice,
    corner_lat,
    slot_lat,
    up_send,
    down_send,
    low_recv,
    high_recv,
    rs_send,
    rs_recv,
    outbuf,
    fetch_sem,
    out_sem,
    c_send_sem,
    c_recv_sem,
    r_send_sem,
    r_recv_sem,
    up_send_sem,
    up_recv_sem,
    down_send_sem,
    down_recv_sem,
):
    op = lax.axis_index("op")
    cell = lax.axis_index("cell")
    n_cell = 128
    nxt = lax.rem(cell + 1, n_cell)
    prv = lax.rem(cell + n_cell - 1, n_cell)
    peers = [lax.rem(op + j, N_OP) for j in range(1, N_OP)]

    fetches = []
    pairs = (
        (coords_in, coords_ref),
        (nodes_in, nodes_ref),
        (adjacency_in, adjacency_ref),
        (send_in, send_ref),
        (start_in, start_ref),
        (jac_in, jac_ref),
        (damp_in, damp_ref),
        (freq_in, freq_ref),
        (objective_in, objective_ref),
        (state_in, state_ref),
    )
    for j, (source, target) in enumerate(pairs):
        fetch = pltpu.make_async_copy(source, target, fetch_sem.at[j])
        fetch.start()
        fetches.append(fetch)

    barrier = pltpu.get_barrier_semaphore()
    for peer in peers:
        pl.semaphore_signal(barrier, inc=1, device_id=(peer, cell), device_id_type=MESH)
    for block in (prv, nxt):
        pl.semaphore_signal(barrier, inc=1, device_id=(op, block), device_id_type=MESH)
    pl.semaphore_wait(barrier, 5)
    fetches[0].wait()

    coord_copies = []
    for j, peer in enumerate(peers):
        copy = pltpu.make_async_remote_copy(
            src_ref=coords_ref,
            dst_ref=cbuf.at[op],
            send_sem=c_send_sem.at[j],
            recv_sem=c_recv_sem.at[j],
            device_id=(peer, cell),
            device_id_type=MESH,
        )
        copy.start()
        coord_copies.append(copy)
    cbuf[op] = coords_ref[...]

    sub = lax.broadcasted_iota(jnp.int32, (8, LANES), 0)
    lane = lax.broadcasted_iota(jnp.int32, (8, LANES), 1)
    layer = sub // 2
    first_op = lax.rem(sub, 2) == 0
    axial = lax.rem(lane, 4)
    for fetch in fetches[1:]:
        fetch.wait()
    stack[48:56, :] = jnp.zeros((8, CELLS_HERE), jnp.float32)
    stack[80:88, :] = jnp.zeros((8, CELLS_HERE), jnp.float32)
    stack_late[96:104, :] = jnp.zeros((8, CELLS_HERE), jnp.float32)
    for j in range(STATE):
        stack[2 * j : 2 * j + 2, :] = start_ref[j]
        stack_late[2 * j : 2 * j + 2, :] = objective_ref[j]
        stack_late[50 + 2 * j : 52 + 2 * j, :] = state_ref[j]
    stack[80:86, :] = adjacency_ref[...].astype(jnp.float32)
    stack[88:96, :] = nodes_ref[...].astype(jnp.float32)

    def pick(p0, p1):
        return jnp.where(first_op, p0, p1)

    jac = [
        [[pick(jac_ref[d, u, 0, v], jac_ref[d, u, 1, v]) for v in range(VARS)] for u in range(VARS)]
        for d in range(3)
    ]
    damp = pick(damp_ref[0], damp_ref[1])
    freq = pick(freq_ref[0], freq_ref[1])

    for copy in coord_copies:
        copy.wait()

    for o in range(N_OP):
        for d in range(3):
            for h in range(2):
                nodebuf[d, 2 * o + h : 2 * o + h + 1, :] = cbuf[
                    o, d : d + 1, h * LANES : (h + 1) * LANES
                ]

    for tile in range(4):
        index = nodes_ref[:, tile * LANES : (tile + 1) * LANES]
        page = index // LANES
        within = lax.rem(index, LANES)
        for d in range(3):
            value = jnp.zeros((8, LANES), jnp.float32)
            for n in range(8):
                got = lanes_at(spread(nodebuf[d, n : n + 1, :]), within)
                value = jnp.where(page == n, got, value)
            stack[56 + 8 * d : 64 + 8 * d, tile * LANES : (tile + 1) * LANES] = value

    base = [jnp.floor(stack[56 + 8 * d : 57 + 8 * d, :] + 0.5).astype(jnp.int32) for d in range(3)]
    pos = base[0] * LANES + base[1] * 4 + base[2]
    onehot = (
        (lax.broadcasted_iota(jnp.int32, (CELLS_HERE, CELLS_HERE), 0) == pos)
        .astype(jnp.float32)
        .astype(jnp.bfloat16)
    )
    moved = move_cells(stack[...], onehot, 1)

    def to_lattice(array, rows, base_row):
        for j in range(STATE):
            row = base_row + 2 * j
            for l in range(4):
                lattice[array, j, 2 * l : 2 * l + 2, :] = rows[
                    row : row + 2, l * LANES : (l + 1) * LANES
                ]

    to_lattice(0, moved, 0)
    for l in range(4):
        for d in range(3):
            part = moved[56 + 8 * d : 64 + 8 * d, l * LANES : (l + 1) * LANES]
            corner_lat[d, :, 2 * l, :] = part
            corner_lat[d, :, 2 * l + 1, :] = part
        slot_lat[:, l, :] = moved[88:96, l * LANES : (l + 1) * LANES]

    def pos_of(cells):
        page = cells // LANES
        within = lax.rem(cells, LANES)
        value = jnp.zeros((8, LANES), jnp.int32)
        for n in range(4):
            got = lanes_at(spread(pos[:, n * LANES : (n + 1) * LANES]), within)
            value = jnp.where(page == n, got, value)
        return lax.rem(value, LANES)

    lower_map = pos_of(spread(send_ref[0:1, :]))
    upper_map = pos_of(spread(send_ref[1:2, :]))

    def pack(values, source):
        packed = []
        for g in range(GROUPS):
            total = values[4 * g]
            for r in range(1, 4):
                if 4 * g + r < STATE:
                    total = jnp.where(
                        layer == (source + r) % 4, pltpu.roll(values[4 * g + r], 2 * r, 0), total
                    )
            packed.append(total)
        return packed

    def exchange(number):
        used = pl.ds(0, GROUPS + 1 if number == 0 else GROUPS)
        up = pltpu.make_async_remote_copy(
            src_ref=up_send.at[number, used],
            dst_ref=low_recv.at[number, used],
            send_sem=up_send_sem.at[number],
            recv_sem=up_recv_sem.at[number],
            device_id=(op, nxt),
            device_id_type=MESH,
        )
        down = pltpu.make_async_remote_copy(
            src_ref=down_send.at[number, used],
            dst_ref=high_recv.at[number, used],
            send_sem=down_send_sem.at[number],
            recv_sem=down_recv_sem.at[number],
            device_id=(op, prv),
            device_id_type=MESH,
        )
        up.start()
        down.start()
        return up, down

    def fill(number, upward, downward):
        for g, value in enumerate(pack(upward, 3)):
            up_send[number, g] = value
        for g, value in enumerate(pack(downward, 0)):
            down_send[number, g] = value

    up_send[0, GROUPS] = upper_map.astype(jnp.float32)
    down_send[0, GROUPS] = lower_map.astype(jnp.float32)

    corner = [[corner_lat[d, c] for d in range(3)] for c in range(8)]
    center = [sum(corner[c][d] for c in range(8)) * 0.125 for d in range(3)]
    normals, areas, offsets = [], [], []
    volume = jnp.zeros((8, LANES), jnp.float32)
    for c0, c1, c2, c3 in FACE_CORNERS:
        first = [corner[c2][d] - corner[c0][d] for d in range(3)]
        second = [corner[c3][d] - corner[c1][d] for d in range(3)]
        normal = [0.5 * x for x in cross(first, second)]
        offset = [
            0.25 * (corner[c0][d] + corner[c1][d] + corner[c2][d] + corner[c3][d]) - center[d]
            for d in range(3)
        ]
        volume = volume + sum(offset[d] * normal[d] for d in range(3))
        normals.append(normal)
        offsets.append(offset)
        areas.append(jnp.sqrt(sum(normal[d] * normal[d] for d in range(3))))
    volume = volume * (1.0 / 3.0)
    area_sum = sum(areas)
    normal_total = [sum(normals[k][d] for k in range(6)) for d in range(3)]
    step = COURANT / ((1.0 + damp) * area_sum + 2.0 * freq * volume)

    inner = [None, None, lane >= 4, lane < LANES - 4, axial > 0, axial < 3]
    face_normal, face_area = [], []
    for k in range(6):
        keep = [0.5 * normals[k][d] for d in range(3)]
        area = 0.5 * damp * areas[k]
        if inner[k] is not None:
            keep = [jnp.where(inner[k], x, 0.0) for x in keep]
            area = jnp.where(inner[k], area, 0.0)
        face_normal.append(keep)
        face_area.append(area)
    half_total = [0.5 * normal_total[d] for d in range(3)]
    self_area = 0.5 * damp * area_sum
    freq_volume = freq * volume
    spectral = spectral_values()

    ghost_index = [None, None]

    def ghosts(number):
        low, high = [], []
        for g in range(GROUPS):
            from_low = lanes_at(low_recv[number, g], ghost_index[0])
            from_high = lanes_at(high_recv[number, g], ghost_index[1])
            for r in range(4):
                if 4 * g + r < STATE:
                    low.append(pltpu.roll(from_low, (2 - 2 * r) % 8, 0))
                    high.append(pltpu.roll(from_high, (6 - 2 * r) % 8, 0))
        return low, high

    def turn(values):
        return [
            [
                sum(jac[d][u][v] * values[t * VARS + u] for u in range(VARS))
                for t in range(INST)
                for v in range(VARS)
            ]
            for d in range(3)
        ]

    adjoint = [lattice[0, j] for j in range(STATE)]
    for sweep in range(ITERS):
        turned = turn(adjoint)

        def outgoing(k, j):
            return (
                face_normal[k][0] * turned[0][j]
                + face_normal[k][1] * turned[1][j]
                + face_normal[k][2] * turned[2][j]
                - face_area[k] * adjoint[j]
            )

        upward = [outgoing(1, j) for j in range(STATE)]
        downward = [outgoing(0, j) for j in range(STATE)]
        fill(sweep, upward, downward)
        pair = exchange(sweep)
        if sweep == 0:
            moved_late = move_cells(stack_late[...], onehot, 1)
            to_lattice(1, moved_late, 0)
            to_lattice(2, moved_late, 50)
            flow = [lattice[2, j] for j in range(STATE)]
            fill(ITERS, flow, flow)
            flow_pair = exchange(ITERS)
        updates = []
        for j in range(STATE):
            t, v = j // VARS, j % VARS
            update = (
                half_total[0] * turned[0][j]
                + half_total[1] * turned[1][j]
                + half_total[2] * turned[2][j]
                + self_area * adjoint[j]
                + lattice[1, j]
            )
            mix = None
            for other in range(INST):
                if other != t:
                    term = float(spectral[other, t]) * adjoint[other * VARS + v]
                    mix = term if mix is None else mix + term
            update = update + freq_volume * mix
            update = update + pltpu.roll(outgoing(3, j), 4, 1)
            update = update + pltpu.roll(outgoing(2, j), LANES - 4, 1)
            update = update + pltpu.roll(outgoing(5, j), 1, 1)
            update = update + pltpu.roll(outgoing(4, j), LANES - 1, 1)
            update = update + jnp.where(layer == 0, 0.0, pltpu.roll(upward[j], 2, 0))
            update = update + jnp.where(layer == 3, 0.0, pltpu.roll(downward[j], 6, 0))
            updates.append(adjoint[j] - step * update)
        for copy in pair:
            copy.wait()
        if sweep == 0:
            for side in range(2):
                table = (low_recv, high_recv)[side][0, GROUPS].astype(jnp.int32)
                tile = 3 * side
                row = moved[80 + side : 81 + side, tile * LANES : (tile + 1) * LANES]
                named = spread(row.astype(jnp.int32)) - CELLS_HERE - side * LANES
                ghost_index[side] = lanes_at(table, jnp.clip(named, 0, LANES - 1))
        low, high = ghosts(sweep)
        adjoint = [
            updates[j] - step * jnp.where(layer == 0, low[j], jnp.where(layer == 3, high[j], 0.0))
            for j in range(STATE)
        ]

    for copy in flow_pair:
        copy.wait()

    low, high = ghosts(ITERS)
    final_rows = turn(adjoint)
    along = [[None] * 3 for _ in range(6)]
    spread_sum = [None] * 6
    here = [None] * 3
    here_damp = None
    volume_sum = None

    def added(total, term):
        return term if total is None else total + term

    for t in range(INST):
        for v in range(VARS):
            j = t * VARS + v
            value = adjoint[j]
            own = lattice[2, j]
            final = [final_rows[d][j] for d in range(3)]
            mix = None
            for other in range(INST):
                if other != t:
                    mix = added(mix, float(spectral[t, other]) * lattice[2, other * VARS + v])
            volume_sum = added(volume_sum, value * mix)
            for d in range(3):
                here[d] = added(here[d], final[d] * own)
            here_damp = added(here_damp, value * own)
            far = [
                jnp.where(layer == 0, low[j], pltpu.roll(own, 2, 0)),
                jnp.where(layer == 3, high[j], pltpu.roll(own, 6, 0)),
                pltpu.roll(own, 4, 1),
                pltpu.roll(own, LANES - 4, 1),
                pltpu.roll(own, 1, 1),
                pltpu.roll(own, LANES - 1, 1),
            ]
            for k in range(6):
                for d in range(3):
                    along[k][d] = added(along[k][d], final[d] * far[k])
                spread_sum[k] = added(spread_sum[k], value * far[k])

    def both(x):
        return x + jnp.where(first_op, pltpu.roll(x, 7, 0), pltpu.roll(x, 1, 0))

    volume_grad = both(volume_sum * freq) * (WEIGHT / 3.0)
    cots = [[None] * 3 for _ in range(8)]
    center_cot = [-(0.125) * volume_grad * normal_total[d] for d in range(3)]
    for k, (c0, c1, c2, c3) in enumerate(FACE_CORNERS):
        far_along, far_damp = along[k], spread_sum[k]
        if inner[k] is not None:
            far_along = [jnp.where(inner[k], x, 0.0) for x in far_along]
            far_damp = jnp.where(inner[k], far_damp, 0.0)
        scale = both(damp * (here_damp - far_damp)) / areas[k]
        grad = [
            (0.5 * WEIGHT) * (both(here[d] + far_along[d]) + scale * normals[k][d])
            + volume_grad * offsets[k][d]
            for d in range(3)
        ]
        first = [corner[c2][d] - corner[c0][d] for d in range(3)]
        second = [corner[c3][d] - corner[c1][d] for d in range(3)]
        to_first = cross(second, grad)
        to_second = cross(grad, first)
        for d in range(3):
            middle = 0.25 * volume_grad * normals[k][d]
            cots[c0][d] = added(cots[c0][d], middle - 0.5 * to_first[d])
            cots[c2][d] = added(cots[c2][d], middle + 0.5 * to_first[d])
            cots[c1][d] = added(cots[c1][d], middle - 0.5 * to_second[d])
            cots[c3][d] = added(cots[c3][d], middle + 0.5 * to_second[d])
    cots = [[cots[c][d] + center_cot[d] for d in range(3)] for c in range(8)]

    def meet(bit, down, up, at_low, at_high):
        for c in range(8):
            if not c & bit:
                for d in range(3):
                    a, b = cots[c][d], cots[c | bit][d]
                    cots[c][d] = a + jnp.where(at_low, 0.0, down(b))
                    cots[c | bit][d] = b + jnp.where(at_high, 0.0, up(a))

    meet(1, lambda x: pltpu.roll(x, 1, 1), lambda x: pltpu.roll(x, LANES - 1, 1), axial == 0, axial == 3)
    meet(2, lambda x: pltpu.roll(x, 4, 1), lambda x: pltpu.roll(x, LANES - 4, 1), lane < 4, lane >= LANES - 4)
    meet(4, lambda x: pltpu.roll(x, 2, 0), lambda x: pltpu.roll(x, 6, 0), layer == 0, layer == 3)

    limits = (4, 32, 4)
    point = [
        jnp.clip(jnp.floor(jnp.clip(nodebuf[d], -1.0, 40.0) + 0.5).astype(jnp.int32), 0, limits[d])
        for d in range(3)
    ]
    home = [jnp.minimum(point[d], limits[d] - 1) for d in range(3)]
    source = ((point[0] - home[0]) * 4 + (point[1] - home[1]) * 2 + point[2] - home[2]) * 4 + home[0]
    within = home[1] * 4 + home[2]
    slot_number = sub * LANES + lane
    sens = [jnp.zeros((8, LANES), jnp.float32) for _ in range(3)]
    for c in range(8):
        slots = slot_lat[c]
        for l in range(4):
            name = lanes_at(spread(slots[l : l + 1]), within).astype(jnp.int32)
            chosen = jnp.logical_and(source == c * 4 + l, name == slot_number)
            for d in range(3):
                got = lanes_at(spread(cots[c][d][2 * l : 2 * l + 1]), within)
                sens[d] = jnp.where(chosen, got, sens[d])

    rs_send[...] = jnp.zeros_like(rs_send)
    for o in range(N_OP):
        for d in range(3):
            rs_send[o, 2 * d : 2 * d + 2, :] = sens[d][2 * o : 2 * o + 2]
    sums = []
    for j, peer in enumerate(peers):
        copy = pltpu.make_async_remote_copy(
            src_ref=rs_send.at[peer],
            dst_ref=rs_recv.at[j],
            send_sem=r_send_sem.at[j],
            recv_sem=r_recv_sem.at[j],
            device_id=(peer, cell),
            device_id_type=MESH,
        )
        copy.start()
        sums.append(copy)

    outbuf[48:56, :] = jnp.zeros((8, CELLS_HERE), jnp.float32)
    for j in range(STATE):
        for l in range(4):
            outbuf[2 * j : 2 * j + 2, l * LANES : (l + 1) * LANES] = adjoint[j][2 * l : 2 * l + 2]
    back = move_cells(outbuf[...], onehot, 0)
    for j in range(STATE):
        out_ref[j] = back[2 * j : 2 * j + 2]
    put = pltpu.make_async_copy(out_ref, out_hbm, out_sem)
    put.start()

    total = rs_send[op]
    for j, copy in enumerate(sums):
        copy.wait()
        total = total + rs_recv[j]
    for d in range(3):
        for h in range(2):
            sens_ref[d : d + 1, h * LANES : (h + 1) * LANES] = total[2 * d + h : 2 * d + h + 1]
    put.wait()


def per_device(
    flow_state,
    adjoint_start,
    objective_grad,
    adjacency,
    send_list,
    cell_nodes,
    coords,
    jacobians,
    dissipation,
    frequency,
):
    anywhere = pl.BlockSpec(memory_space=pl.ANY)
    f32, i32 = jnp.float32, jnp.int32
    dma = pltpu.SemaphoreType.DMA

    def pairs(x):
        return x.transpose(1, 2, 0, 3).reshape(STATE, OPS_HERE, CELLS_HERE)

    rows = pltpu.VMEM((STATE, OPS_HERE, CELLS_HERE), f32)
    message = pltpu.VMEM((ITERS + 1, GROUPS + 1, 8, LANES), f32)
    adjoint, sens = pl.pallas_call(
        kernel,
        out_shape=(
            jax.ShapeDtypeStruct((STATE, OPS_HERE, CELLS_HERE), f32),
            jax.ShapeDtypeStruct(coords.shape, f32),
        ),
        in_specs=[anywhere] * 10,
        out_specs=(anywhere, pl.BlockSpec(memory_space=pltpu.VMEM)),
        scratch_shapes=[
            rows,
            rows,
            rows,
            pltpu.VMEM((6, CELLS_HERE), i32),
            pltpu.VMEM((2, LANES), i32),
            pltpu.VMEM((8, CELLS_HERE), i32),
            pltpu.VMEM((3, 256), f32),
            pltpu.SMEM((3, VARS, OPS_HERE, VARS), f32),
            pltpu.SMEM((OPS_HERE,), f32),
            pltpu.SMEM((OPS_HERE,), f32),
            rows,
            pltpu.VMEM((N_OP, 3, 256), f32),
            pltpu.VMEM((3, 8, LANES), f32),
            pltpu.VMEM((96, CELLS_HERE), f32),
            pltpu.VMEM((104, CELLS_HERE), f32),
            pltpu.VMEM((3, STATE, 8, LANES), f32),
            pltpu.VMEM((3, 8, 8, LANES), f32),
            pltpu.VMEM((8, 8, LANES), f32),
            message,
            message,
            message,
            message,
            pltpu.VMEM((N_OP, 8, LANES), f32),
            pltpu.VMEM((N_OP - 1, 8, LANES), f32),
            pltpu.VMEM((56, CELLS_HERE), f32),
            dma((10,)),
            dma,
            dma((3,)),
            dma((3,)),
            dma((3,)),
            dma((3,)),
            dma((ITERS + 1,)),
            dma((ITERS + 1,)),
            dma((ITERS + 1,)),
            dma((ITERS + 1,)),
        ],
        compiler_params=pltpu.CompilerParams(collective_id=0, has_side_effects=True),
    )(
        pairs(flow_state),
        pairs(adjoint_start),
        pairs(objective_grad),
        adjacency,
        send_list.reshape(2, LANES),
        cell_nodes,
        coords,
        jacobians.transpose(1, 2, 0, 3),
        dissipation,
        frequency,
    )
    adjoint = adjoint.reshape(INST, VARS, OPS_HERE, CELLS_HERE).transpose(2, 0, 1, 3)
    return adjoint, sens


def solution(mesh):
    in_specs = (
        P("op", None, None, "cell"),
        P("op", None, None, "cell"),
        P("op", None, None, "cell"),
        P(None, "cell"),
        P("cell"),
        P(None, "cell"),
        P(None, ("op", "cell")),
        P("op", None, None, None),
        P("op"),
        P("op"),
    )
    out_specs = (P("op", None, None, "cell"), P(None, ("op", "cell")))
    return jax.shard_map(
        per_device, mesh=mesh, in_specs=in_specs, out_specs=out_specs, check_vma=False
    )
```

```python
import functools
import math

import jax
import jax.numpy as jnp
import numpy as np
from jax import lax
from jax.experimental import pallas as pl
from jax.experimental.pallas import tpu as pltpu
from jax.sharding import PartitionSpec as P

ITERS = 4
INST = 5
VARS = 5
OPS_HERE = 2
N_OP = 4
LANES = 128
CELLS_HERE = 512
FACE_CORNERS = ((0, 1, 3, 2), (4, 6, 7, 5), (0, 4, 5, 1), (2, 3, 7, 6), (0, 2, 6, 4), (1, 5, 7, 3))
COURANT = 1.2
WEIGHT = 1.0 / 8
STATE = INST * VARS
GROUPS = (STATE + 3) // 4
MESH = pl.DeviceIdType.MESH


def spectral_values():
    values = np.zeros((INST, INST))
    for t in range(INST):
        for s in range(INST):
            if t != s:
                values[t, s] = 0.5 * (-1.0) ** (t - s) / math.sin(math.pi * (t - s) / INST)
    return values


def lanes_at(table, index):
    return jnp.take_along_axis(table, index, axis=1, mode="promise_in_bounds")


def split3(x):
    hi = x.astype(jnp.bfloat16)
    rest = x - hi.astype(jnp.float32)
    mid = rest.astype(jnp.bfloat16)
    low = (rest - mid.astype(jnp.float32)).astype(jnp.bfloat16)
    return jnp.concatenate([hi, mid, low], axis=0)


def move_cells(x, onehot, contract):
    rows = x.shape[0]
    y = lax.dot_general(
        split3(x), onehot, (((1,), (contract,)), ((), ())), preferred_element_type=jnp.float32
    )
    return y[:rows] + y[rows : 2 * rows] + y[2 * rows :]


def spread(row):
    return jnp.broadcast_to(row, (8, LANES))


def cross(a, b):
    return [a[1] * b[2] - a[2] * b[1], a[2] * b[0] - a[0] * b[2], a[0] * b[1] - a[1] * b[0]]


def kernel(
    state_in,
    start_in,
    objective_in,
    adjacency_in,
    send_in,
    nodes_in,
    coords_in,
    jac_in,
    damp_in,
    freq_in,
    out_hbm,
    sens_ref,
    state_ref,
    start_ref,
    objective_ref,
    adjacency_ref,
    send_ref,
    nodes_ref,
    coords_ref,
    jac_ref,
    damp_ref,
    freq_ref,
    out_ref,
    cbuf,
    nodebuf,
    stack,
    stack_late,
    lattice,
    corner_lat,
    slot_lat,
    up_send,
    down_send,
    low_recv,
    high_recv,
    map_up,
    map_down,
    map_low,
    map_high,
    low_state,
    high_state,
    low_corner,
    high_corner,
    rs_send,
    rs_recv,
    outbuf,
    fetch_sem,
    out_sem,
    c_send_sem,
    c_recv_sem,
    r_send_sem,
    r_recv_sem,
    up_send_sem,
    up_recv_sem,
    down_send_sem,
    down_recv_sem,
):
    op = lax.axis_index("op")
    cell = lax.axis_index("cell")
    n_cell = 128
    nxt = lax.rem(cell + 1, n_cell)
    prv = lax.rem(cell + n_cell - 1, n_cell)
    peers = [lax.rem(op + j, N_OP) for j in range(1, N_OP)]

    fetches = []
    pairs = (
        (coords_in, coords_ref),
        (nodes_in, nodes_ref),
        (adjacency_in, adjacency_ref),
        (send_in, send_ref),
        (start_in, start_ref),
        (jac_in, jac_ref),
        (damp_in, damp_ref),
        (freq_in, freq_ref),
        (objective_in, objective_ref),
        (state_in, state_ref),
    )
    for j, (source, target) in enumerate(pairs):
        fetch = pltpu.make_async_copy(source, target, fetch_sem.at[j])
        fetch.start()
        fetches.append(fetch)

    barrier = pltpu.get_barrier_semaphore()
    for peer in peers:
        pl.semaphore_signal(barrier, inc=1, device_id=(peer, cell), device_id_type=MESH)
    for block in (prv, nxt):
        pl.semaphore_signal(barrier, inc=1, device_id=(op, block), device_id_type=MESH)
    pl.semaphore_wait(barrier, 5)
    fetches[0].wait()

    coord_copies = []
    for j, peer in enumerate(peers):
        copy = pltpu.make_async_remote_copy(
            src_ref=coords_ref,
            dst_ref=cbuf.at[op],
            send_sem=c_send_sem.at[j],
            recv_sem=c_recv_sem.at[j],
            device_id=(peer, cell),
            device_id_type=MESH,
        )
        copy.start()
        coord_copies.append(copy)
    cbuf[op] = coords_ref[...]

    sub = lax.broadcasted_iota(jnp.int32, (8, LANES), 0)
    lane = lax.broadcasted_iota(jnp.int32, (8, LANES), 1)
    layer = sub // 2
    first_op = lax.rem(sub, 2) == 0
    axial = lax.rem(lane, 4)
    for fetch in fetches[1:]:
        fetch.wait()
    stack[48:56, :] = jnp.zeros((8, CELLS_HERE), jnp.float32)
    stack[80:88, :] = jnp.zeros((8, CELLS_HERE), jnp.float32)
    stack_late[96:104, :] = jnp.zeros((8, CELLS_HERE), jnp.float32)
    for j in range(STATE):
        stack[2 * j : 2 * j + 2, :] = start_ref[j]
        stack_late[2 * j : 2 * j + 2, :] = objective_ref[j]
        stack_late[50 + 2 * j : 52 + 2 * j, :] = state_ref[j]
    stack[80:86, :] = adjacency_ref[...].astype(jnp.float32)
    stack[88:96, :] = nodes_ref[...].astype(jnp.float32)

    def pick(p0, p1):
        return jnp.where(first_op, p0, p1)

    jac = [
        [[pick(jac_ref[d, u, 0, v], jac_ref[d, u, 1, v]) for v in range(VARS)] for u in range(VARS)]
        for d in range(3)
    ]
    damp = pick(damp_ref[0], damp_ref[1])
    freq = pick(freq_ref[0], freq_ref[1])

    for copy in coord_copies:
        copy.wait()

    for o in range(N_OP):
        for d in range(3):
            for h in range(2):
                nodebuf[d, 2 * o + h : 2 * o + h + 1, :] = cbuf[
                    o, d : d + 1, h * LANES : (h + 1) * LANES
                ]

    for tile in range(4):
        index = nodes_ref[:, tile * LANES : (tile + 1) * LANES]
        page = index // LANES
        within = lax.rem(index, LANES)
        for d in range(3):
            value = jnp.zeros((8, LANES), jnp.float32)
            for n in range(8):
                got = lanes_at(spread(nodebuf[d, n : n + 1, :]), within)
                value = jnp.where(page == n, got, value)
            stack[56 + 8 * d : 64 + 8 * d, tile * LANES : (tile + 1) * LANES] = value

    base = [jnp.floor(stack[56 + 8 * d : 57 + 8 * d, :] + 0.5).astype(jnp.int32) for d in range(3)]
    pos = base[0] * LANES + base[1] * 4 + base[2]
    onehot = (
        (lax.broadcasted_iota(jnp.int32, (CELLS_HERE, CELLS_HERE), 0) == pos)
        .astype(jnp.float32)
        .astype(jnp.bfloat16)
    )
    moved = move_cells(stack[...], onehot, 1)

    def to_lattice(array, rows, base_row):
        for j in range(STATE):
            row = base_row + 2 * j
            for l in range(4):
                lattice[array, j, 2 * l : 2 * l + 2, :] = rows[
                    row : row + 2, l * LANES : (l + 1) * LANES
                ]

    to_lattice(0, moved, 0)
    for l in range(4):
        for d in range(3):
            part = moved[56 + 8 * d : 64 + 8 * d, l * LANES : (l + 1) * LANES]
            corner_lat[d, :, 2 * l, :] = part
            corner_lat[d, :, 2 * l + 1, :] = part
        slot_lat[:, l, :] = moved[88:96, l * LANES : (l + 1) * LANES]

    def pos_of(cells):
        page = cells // LANES
        within = lax.rem(cells, LANES)
        value = jnp.zeros((8, LANES), jnp.int32)
        for n in range(4):
            got = lanes_at(spread(pos[:, n * LANES : (n + 1) * LANES]), within)
            value = jnp.where(page == n, got, value)
        return lax.rem(value, LANES)

    lower_map = pos_of(spread(send_ref[0:1, :]))
    upper_map = pos_of(spread(send_ref[1:2, :]))

    def pack(values, source):
        packed = []
        for g in range(GROUPS):
            total = values[4 * g]
            for r in range(1, 4):
                if 4 * g + r < STATE:
                    total = jnp.where(
                        layer == (source + r) % 4, pltpu.roll(values[4 * g + r], 2 * r, 0), total
                    )
            packed.append(total)
        return packed

    def exchange(number, up_from, low_to, down_from, high_to):
        up = pltpu.make_async_remote_copy(
            src_ref=up_from,
            dst_ref=low_to,
            send_sem=up_send_sem.at[number],
            recv_sem=up_recv_sem.at[number],
            device_id=(op, nxt),
            device_id_type=MESH,
        )
        down = pltpu.make_async_remote_copy(
            src_ref=down_from,
            dst_ref=high_to,
            send_sem=down_send_sem.at[number],
            recv_sem=down_recv_sem.at[number],
            device_id=(op, prv),
            device_id_type=MESH,
        )
        up.start()
        down.start()
        copies.extend((up, down))

    copies = []

    def end_names(side):
        tile = 3 * side
        row = moved[80 + side : 81 + side, tile * LANES : (tile + 1) * LANES]
        named = spread(row.astype(jnp.int32)) - CELLS_HERE - side * LANES
        return jnp.clip(named, 0, LANES - 1)

    low_names, high_names = end_names(0), end_names(1)
    map_up[0] = upper_map.astype(jnp.float32)
    map_up[1] = high_names.astype(jnp.float32)
    map_down[0] = lower_map.astype(jnp.float32)
    map_down[1] = low_names.astype(jnp.float32)
    exchange(0, lattice.at[0], low_state.at[0], lattice.at[0], high_state.at[0])
    exchange(1, corner_lat, low_corner, corner_lat, high_corner)
    exchange(2, map_up, map_low, map_down, map_high)
    moved_late = move_cells(stack_late[...], onehot, 1)
    to_lattice(1, moved_late, 0)
    exchange(3, lattice.at[1], low_state.at[1], lattice.at[1], high_state.at[1])
    to_lattice(2, moved_late, 50)
    flow = [lattice[2, j] for j in range(STATE)]
    for g, value in enumerate(pack(flow, 3)):
        up_send[g] = value
    for g, value in enumerate(pack(flow, 0)):
        down_send[g] = value
    exchange(4, up_send, low_recv, down_send, high_recv)

    inner = [None, None, lane >= 4, lane < LANES - 4, axial > 0, axial < 3]

    def geometry(points):
        corner = [[points[d, c] for d in range(3)] for c in range(8)]
        center = [sum(corner[c][d] for c in range(8)) * 0.125 for d in range(3)]
        normals, areas, offsets = [], [], []
        volume = jnp.zeros((8, LANES), jnp.float32)
        for c0, c1, c2, c3 in FACE_CORNERS:
            first = [corner[c2][d] - corner[c0][d] for d in range(3)]
            second = [corner[c3][d] - corner[c1][d] for d in range(3)]
            normal = [0.5 * x for x in cross(first, second)]
            offset = [
                0.25 * (corner[c0][d] + corner[c1][d] + corner[c2][d] + corner[c3][d]) - center[d]
                for d in range(3)
            ]
            volume = volume + sum(offset[d] * normal[d] for d in range(3))
            normals.append(normal)
            offsets.append(offset)
            areas.append(jnp.sqrt(sum(normal[d] * normal[d] for d in range(3))))
        volume = volume * (1.0 / 3.0)
        area_sum = sum(areas)
        normal_total = [sum(normals[k][d] for k in range(6)) for d in range(3)]
        step = COURANT / ((1.0 + damp) * area_sum + 2.0 * freq * volume)
        face_normal, face_area = [], []
        for k in range(6):
            keep = [0.5 * normals[k][d] for d in range(3)]
            area = 0.5 * damp * areas[k]
            if inner[k] is not None:
                keep = [jnp.where(inner[k], x, 0.0) for x in keep]
                area = jnp.where(inner[k], area, 0.0)
            face_normal.append(keep)
            face_area.append(area)
        half_total = [0.5 * normal_total[d] for d in range(3)]
        sweep_terms = (face_normal, face_area, half_total, 0.5 * damp * area_sum, freq * volume, step)
        return sweep_terms, (corner, normals, areas, offsets, normal_total)

    own_terms, (corner, normals, areas, offsets, normal_total) = geometry(corner_lat)
    spectral = spectral_values()

    def ghosts():
        low, high = [], []
        for g in range(GROUPS):
            from_low = lanes_at(low_recv[g], ghost_index[0])
            from_high = lanes_at(high_recv[g], ghost_index[1])
            for r in range(4):
                if 4 * g + r < STATE:
                    low.append(pltpu.roll(from_low, (2 - 2 * r) % 8, 0))
                    high.append(pltpu.roll(from_high, (6 - 2 * r) % 8, 0))
        return low, high

    def turn(values):
        return [
            [
                sum(jac[d][u][v] * values[t * VARS + u] for u in range(VARS))
                for t in range(INST)
                for v in range(VARS)
            ]
            for d in range(3)
        ]

    for copy in copies:
        copy.wait()

    ghost_index = [
        lanes_at(map_low[0].astype(jnp.int32), low_names),
        lanes_at(map_high[0].astype(jnp.int32), high_names),
    ]
    from_low_index = lanes_at(lower_map, map_low[1].astype(jnp.int32))
    from_high_index = lanes_at(upper_map, map_high[1].astype(jnp.int32))
    low_terms, _ = geometry(low_corner)
    high_terms, _ = geometry(high_corner)

    def outgoing(terms, k, turned, adjoint, j):
        face_normal, face_area = terms[:2]
        return (
            face_normal[k][0] * turned[0][j]
            + face_normal[k][1] * turned[1][j]
            + face_normal[k][2] * turned[2][j]
            - face_area[k] * adjoint[j]
        )

    def update_inside(terms, turned, adjoint, objective, j):
        _, _, half_total, self_area, freq_volume, _ = terms
        t, v = j // VARS, j % VARS
        update = (
            half_total[0] * turned[0][j]
            + half_total[1] * turned[1][j]
            + half_total[2] * turned[2][j]
            + self_area * adjoint[j]
            + objective[1, j]
        )
        mix = None
        for other in range(INST):
            if other != t:
                term = float(spectral[other, t]) * adjoint[other * VARS + v]
                mix = term if mix is None else mix + term
        update = update + freq_volume * mix
        update = update + pltpu.roll(outgoing(terms, 3, turned, adjoint, j), 4, 1)
        update = update + pltpu.roll(outgoing(terms, 2, turned, adjoint, j), LANES - 4, 1)
        update = update + pltpu.roll(outgoing(terms, 5, turned, adjoint, j), 1, 1)
        return update + pltpu.roll(outgoing(terms, 4, turned, adjoint, j), LANES - 1, 1)

    def sweep_blocks(neighbours_too):
        own = [lattice[0, j] for j in range(STATE)]
        own_turned = turn(own)
        own_up = [pltpu.roll(outgoing(own_terms, 1, own_turned, own, j), 2, 0) for j in range(STATE)]
        own_down = [pltpu.roll(outgoing(own_terms, 0, own_turned, own, j), 6, 0) for j in range(STATE)]

        low = [low_state[0, j] for j in range(STATE)]
        low_turned = turn(low)
        low_up = [pltpu.roll(outgoing(low_terms, 1, low_turned, low, j), 2, 0) for j in range(STATE)]
        if neighbours_too:
            for j in range(STATE):
                near = jnp.where(layer == 0, 0.0, low_up[j])
                down = pltpu.roll(outgoing(low_terms, 0, low_turned, low, j), 6, 0)
                near = near + jnp.where(layer == 3, lanes_at(own_down[j], from_low_index), down)
                update = update_inside(low_terms, low_turned, low, low_state, j) + near
                low_state[0, j] = low[j] - low_terms[5] * update

        high = [high_state[0, j] for j in range(STATE)]
        high_turned = turn(high)
        high_down = [
            pltpu.roll(outgoing(high_terms, 0, high_turned, high, j), 6, 0) for j in range(STATE)
        ]
        if neighbours_too:
            for j in range(STATE):
                near = jnp.where(layer == 3, 0.0, high_down[j])
                up = pltpu.roll(outgoing(high_terms, 1, high_turned, high, j), 2, 0)
                near = near + jnp.where(layer == 0, lanes_at(own_up[j], from_high_index), up)
                update = update_inside(high_terms, high_turned, high, high_state, j) + near
                high_state[0, j] = high[j] - high_terms[5] * update

        for j in range(STATE):
            near = jnp.where(layer == 0, lanes_at(low_up[j], ghost_index[0]), own_up[j])
            near = near + jnp.where(layer == 3, lanes_at(high_down[j], ghost_index[1]), own_down[j])
            update = update_inside(own_terms, own_turned, own, lattice, j) + near
            lattice[0, j] = own[j] - own_terms[5] * update

    def body(sweep, carry):
        sweep_blocks(True)
        return carry

    lax.fori_loop(0, ITERS - 1, body, 0)
    sweep_blocks(False)
    adjoint = [lattice[0, j] for j in range(STATE)]

    low, high = ghosts()
    final_rows = turn(adjoint)
    along = [[None] * 3 for _ in range(6)]
    spread_sum = [None] * 6
    here = [None] * 3
    here_damp = None
    volume_sum = None

    def added(total, term):
        return term if total is None else total + term

    for t in range(INST):
        for v in range(VARS):
            j = t * VARS + v
            value = adjoint[j]
            own = lattice[2, j]
            final = [final_rows[d][j] for d in range(3)]
            mix = None
            for other in range(INST):
                if other != t:
                    mix = added(mix, float(spectral[t, other]) * lattice[2, other * VARS + v])
            volume_sum = added(volume_sum, value * mix)
            for d in range(3):
                here[d] = added(here[d], final[d] * own)
            here_damp = added(here_damp, value * own)
            far = [
                jnp.where(layer == 0, low[j], pltpu.roll(own, 2, 0)),
                jnp.where(layer == 3, high[j], pltpu.roll(own, 6, 0)),
                pltpu.roll(own, 4, 1),
                pltpu.roll(own, LANES - 4, 1),
                pltpu.roll(own, 1, 1),
                pltpu.roll(own, LANES - 1, 1),
            ]
            for k in range(6):
                for d in range(3):
                    along[k][d] = added(along[k][d], final[d] * far[k])
                spread_sum[k] = added(spread_sum[k], value * far[k])

    def both(x):
        return x + jnp.where(first_op, pltpu.roll(x, 7, 0), pltpu.roll(x, 1, 0))

    volume_grad = both(volume_sum * freq) * (WEIGHT / 3.0)
    cots = [[None] * 3 for _ in range(8)]
    center_cot = [-(0.125) * volume_grad * normal_total[d] for d in range(3)]
    for k, (c0, c1, c2, c3) in enumerate(FACE_CORNERS):
        far_along, far_damp = along[k], spread_sum[k]
        if inner[k] is not None:
            far_along = [jnp.where(inner[k], x, 0.0) for x in far_along]
            far_damp = jnp.where(inner[k], far_damp, 0.0)
        scale = both(damp * (here_damp - far_damp)) / areas[k]
        grad = [
            (0.5 * WEIGHT) * (both(here[d] + far_along[d]) + scale * normals[k][d])
            + volume_grad * offsets[k][d]
            for d in range(3)
        ]
        first = [corner[c2][d] - corner[c0][d] for d in range(3)]
        second = [corner[c3][d] - corner[c1][d] for d in range(3)]
        to_first = cross(second, grad)
        to_second = cross(grad, first)
        for d in range(3):
            middle = 0.25 * volume_grad * normals[k][d]
            cots[c0][d] = added(cots[c0][d], middle - 0.5 * to_first[d])
            cots[c2][d] = added(cots[c2][d], middle + 0.5 * to_first[d])
            cots[c1][d] = added(cots[c1][d], middle - 0.5 * to_second[d])
            cots[c3][d] = added(cots[c3][d], middle + 0.5 * to_second[d])
    cots = [[cots[c][d] + center_cot[d] for d in range(3)] for c in range(8)]

    def meet(bit, down, up, at_low, at_high):
        for c in range(8):
            if not c & bit:
                for d in range(3):
                    a, b = cots[c][d], cots[c | bit][d]
                    cots[c][d] = a + jnp.where(at_low, 0.0, down(b))
                    cots[c | bit][d] = b + jnp.where(at_high, 0.0, up(a))

    meet(1, lambda x: pltpu.roll(x, 1, 1), lambda x: pltpu.roll(x, LANES - 1, 1), axial == 0, axial == 3)
    meet(2, lambda x: pltpu.roll(x, 4, 1), lambda x: pltpu.roll(x, LANES - 4, 1), lane < 4, lane >= LANES - 4)
    meet(4, lambda x: pltpu.roll(x, 2, 0), lambda x: pltpu.roll(x, 6, 0), layer == 0, layer == 3)

    limits = (4, 32, 4)
    point = [
        jnp.clip(jnp.floor(jnp.clip(nodebuf[d], -1.0, 40.0) + 0.5).astype(jnp.int32), 0, limits[d])
        for d in range(3)
    ]
    home = [jnp.minimum(point[d], limits[d] - 1) for d in range(3)]
    source = ((point[0] - home[0]) * 4 + (point[1] - home[1]) * 2 + point[2] - home[2]) * 4 + home[0]
    within = home[1] * 4 + home[2]
    slot_number = sub * LANES + lane
    sens = [jnp.zeros((8, LANES), jnp.float32) for _ in range(3)]
    for c in range(8):
        slots = slot_lat[c]
        for l in range(4):
            name = lanes_at(spread(slots[l : l + 1]), within).astype(jnp.int32)
            chosen = jnp.logical_and(source == c * 4 + l, name == slot_number)
            for d in range(3):
                got = lanes_at(spread(cots[c][d][2 * l : 2 * l + 1]), within)
                sens[d] = jnp.where(chosen, got, sens[d])

    rs_send[...] = jnp.zeros_like(rs_send)
    for o in range(N_OP):
        for d in range(3):
            rs_send[o, 2 * d : 2 * d + 2, :] = sens[d][2 * o : 2 * o + 2]
    sums = []
    for j, peer in enumerate(peers):
        copy = pltpu.make_async_remote_copy(
            src_ref=rs_send.at[peer],
            dst_ref=rs_recv.at[j],
            send_sem=r_send_sem.at[j],
            recv_sem=r_recv_sem.at[j],
            device_id=(peer, cell),
            device_id_type=MESH,
        )
        copy.start()
        sums.append(copy)

    outbuf[48:56, :] = jnp.zeros((8, CELLS_HERE), jnp.float32)
    for j in range(STATE):
        for l in range(4):
            outbuf[2 * j : 2 * j + 2, l * LANES : (l + 1) * LANES] = adjoint[j][2 * l : 2 * l + 2]
    back = move_cells(outbuf[...], onehot, 0)
    for j in range(STATE):
        out_ref[j] = back[2 * j : 2 * j + 2]
    put = pltpu.make_async_copy(out_ref, out_hbm, out_sem)
    put.start()

    total = rs_send[op]
    for j, copy in enumerate(sums):
        copy.wait()
        total = total + rs_recv[j]
    for d in range(3):
        for h in range(2):
            sens_ref[d : d + 1, h * LANES : (h + 1) * LANES] = total[2 * d + h : 2 * d + h + 1]
    put.wait()


def per_device(
    flow_state,
    adjoint_start,
    objective_grad,
    adjacency,
    send_list,
    cell_nodes,
    coords,
    jacobians,
    dissipation,
    frequency,
):
    anywhere = pl.BlockSpec(memory_space=pl.ANY)
    f32, i32 = jnp.float32, jnp.int32
    dma = pltpu.SemaphoreType.DMA

    def pairs(x):
        return x.transpose(1, 2, 0, 3).reshape(STATE, OPS_HERE, CELLS_HERE)

    rows = pltpu.VMEM((STATE, OPS_HERE, CELLS_HERE), f32)
    message = pltpu.VMEM((GROUPS, 8, LANES), f32)
    maps = pltpu.VMEM((2, 8, LANES), f32)
    block = pltpu.VMEM((2, STATE, 8, LANES), f32)
    points = pltpu.VMEM((3, 8, 8, LANES), f32)
    adjoint, sens = pl.pallas_call(
        kernel,
        out_shape=(
            jax.ShapeDtypeStruct((STATE, OPS_HERE, CELLS_HERE), f32),
            jax.ShapeDtypeStruct(coords.shape, f32),
        ),
        in_specs=[anywhere] * 10,
        out_specs=(anywhere, pl.BlockSpec(memory_space=pltpu.VMEM)),
        scratch_shapes=[
            rows,
            rows,
            rows,
            pltpu.VMEM((6, CELLS_HERE), i32),
            pltpu.VMEM((2, LANES), i32),
            pltpu.VMEM((8, CELLS_HERE), i32),
            pltpu.VMEM((3, 256), f32),
            pltpu.SMEM((3, VARS, OPS_HERE, VARS), f32),
            pltpu.SMEM((OPS_HERE,), f32),
            pltpu.SMEM((OPS_HERE,), f32),
            rows,
            pltpu.VMEM((N_OP, 3, 256), f32),
            pltpu.VMEM((3, 8, LANES), f32),
            pltpu.VMEM((96, CELLS_HERE), f32),
            pltpu.VMEM((104, CELLS_HERE), f32),
            pltpu.VMEM((3, STATE, 8, LANES), f32),
            pltpu.VMEM((3, 8, 8, LANES), f32),
            pltpu.VMEM((8, 8, LANES), f32),
            message,
            message,
            message,
            message,
            maps,
            maps,
            maps,
            maps,
            block,
            block,
            points,
            points,
            pltpu.VMEM((N_OP, 8, LANES), f32),
            pltpu.VMEM((N_OP - 1, 8, LANES), f32),
            pltpu.VMEM((56, CELLS_HERE), f32),
            dma((10,)),
            dma,
            dma((3,)),
            dma((3,)),
            dma((3,)),
            dma((3,)),
            dma((5,)),
            dma((5,)),
            dma((5,)),
            dma((5,)),
        ],
        compiler_params=pltpu.CompilerParams(collective_id=0, has_side_effects=True),
    )(
        pairs(flow_state),
        pairs(adjoint_start),
        pairs(objective_grad),
        adjacency,
        send_list.reshape(2, LANES),
        cell_nodes,
        coords,
        jacobians.transpose(1, 2, 0, 3),
        dissipation,
        frequency,
    )
    adjoint = adjoint.reshape(INST, VARS, OPS_HERE, CELLS_HERE).transpose(2, 0, 1, 3)
    return adjoint, sens


def solution(mesh):
    in_specs = (
        P("op", None, None, "cell"),
        P("op", None, None, "cell"),
        P("op", None, None, "cell"),
        P(None, "cell"),
        P("cell"),
        P(None, "cell"),
        P(None, ("op", "cell")),
        P("op", None, None, None),
        P("op"),
        P("op"),
    )
    out_specs = (P("op", None, None, "cell"), P(None, ("op", "cell")))
    return jax.shard_map(
        per_device, mesh=mesh, in_specs=in_specs, out_specs=out_specs, check_vma=False
    )
```

```python
import functools
import math

import jax
import jax.numpy as jnp
import numpy as np
from jax import lax
from jax.experimental import pallas as pl
from jax.experimental.pallas import tpu as pltpu
from jax.sharding import PartitionSpec as P

ITERS = 4
INST = 5
VARS = 5
OPS_HERE = 2
N_OP = 4
LANES = 128
CELLS_HERE = 512
FACE_CORNERS = ((0, 1, 3, 2), (4, 6, 7, 5), (0, 4, 5, 1), (2, 3, 7, 6), (0, 2, 6, 4), (1, 5, 7, 3))
COURANT = 1.2
WEIGHT = 1.0 / 8
STATE = INST * VARS
GROUPS = (STATE + 3) // 4
MESH = pl.DeviceIdType.MESH


def spectral_values():
    values = np.zeros((INST, INST))
    for t in range(INST):
        for s in range(INST):
            if t != s:
                values[t, s] = 0.5 * (-1.0) ** (t - s) / math.sin(math.pi * (t - s) / INST)
    return values


def lanes_at(table, index):
    return jnp.take_along_axis(table, index, axis=1, mode="promise_in_bounds")


def split3(x):
    hi = x.astype(jnp.bfloat16)
    rest = x - hi.astype(jnp.float32)
    mid = rest.astype(jnp.bfloat16)
    low = (rest - mid.astype(jnp.float32)).astype(jnp.bfloat16)
    return jnp.concatenate([hi, mid, low], axis=0)


def move_cells(x, onehot, contract):
    rows = x.shape[0]
    y = lax.dot_general(
        split3(x), onehot, (((1,), (contract,)), ((), ())), preferred_element_type=jnp.float32
    )
    return y[:rows] + y[rows : 2 * rows] + y[2 * rows :]


def spread(row):
    return jnp.broadcast_to(row, (8, LANES))


def cross(a, b):
    return [a[1] * b[2] - a[2] * b[1], a[2] * b[0] - a[0] * b[2], a[0] * b[1] - a[1] * b[0]]


def kernel(
    state_in,
    start_in,
    objective_in,
    adjacency_in,
    send_in,
    nodes_in,
    coords_in,
    jac_in,
    damp_in,
    freq_in,
    out_hbm,
    sens_ref,
    state_ref,
    start_ref,
    objective_ref,
    adjacency_ref,
    send_ref,
    nodes_ref,
    coords_ref,
    jac_ref,
    damp_ref,
    freq_ref,
    out_ref,
    cbuf,
    nodebuf,
    stack,
    stack_late,
    lattice,
    corner_lat,
    slot_lat,
    up_send,
    down_send,
    low_recv,
    high_recv,
    map_up,
    map_down,
    map_low,
    map_high,
    low_state,
    high_state,
    low_corner,
    high_corner,
    first_part,
    rs_send,
    rs_recv,
    outbuf,
    fetch_sem,
    out_sem,
    c_send_sem,
    c_recv_sem,
    r_send_sem,
    r_recv_sem,
    up_send_sem,
    up_recv_sem,
    down_send_sem,
    down_recv_sem,
):
    op = lax.axis_index("op")
    cell = lax.axis_index("cell")
    n_cell = 128
    nxt = lax.rem(cell + 1, n_cell)
    prv = lax.rem(cell + n_cell - 1, n_cell)
    peers = [lax.rem(op + j, N_OP) for j in range(1, N_OP)]

    fetches = []
    pairs = (
        (coords_in, coords_ref),
        (nodes_in, nodes_ref),
        (adjacency_in, adjacency_ref),
        (send_in, send_ref),
        (start_in, start_ref),
        (jac_in, jac_ref),
        (damp_in, damp_ref),
        (freq_in, freq_ref),
        (objective_in, objective_ref),
        (state_in, state_ref),
    )
    for j, (source, target) in enumerate(pairs):
        fetch = pltpu.make_async_copy(source, target, fetch_sem.at[j])
        fetch.start()
        fetches.append(fetch)

    barrier = pltpu.get_barrier_semaphore()
    for peer in peers:
        pl.semaphore_signal(barrier, inc=1, device_id=(peer, cell), device_id_type=MESH)
    for block in (prv, nxt):
        pl.semaphore_signal(barrier, inc=1, device_id=(op, block), device_id_type=MESH)
    pl.semaphore_wait(barrier, 5)
    fetches[0].wait()

    coord_copies = []
    for j, peer in enumerate(peers):
        copy = pltpu.make_async_remote_copy(
            src_ref=coords_ref,
            dst_ref=cbuf.at[op],
            send_sem=c_send_sem.at[j],
            recv_sem=c_recv_sem.at[j],
            device_id=(peer, cell),
            device_id_type=MESH,
        )
        copy.start()
        coord_copies.append(copy)
    cbuf[op] = coords_ref[...]

    sub = lax.broadcasted_iota(jnp.int32, (8, LANES), 0)
    lane = lax.broadcasted_iota(jnp.int32, (8, LANES), 1)
    layer = sub // 2
    first_op = lax.rem(sub, 2) == 0
    axial = lax.rem(lane, 4)
    for fetch in fetches[1:]:
        fetch.wait()
    stack[48:56, :] = jnp.zeros((8, CELLS_HERE), jnp.float32)
    stack[80:88, :] = jnp.zeros((8, CELLS_HERE), jnp.float32)
    stack_late[96:104, :] = jnp.zeros((8, CELLS_HERE), jnp.float32)
    for j in range(STATE):
        stack[2 * j : 2 * j + 2, :] = start_ref[j]
        stack_late[2 * j : 2 * j + 2, :] = objective_ref[j]
        stack_late[50 + 2 * j : 52 + 2 * j, :] = state_ref[j]
    stack[80:86, :] = adjacency_ref[...].astype(jnp.float32)
    stack[88:96, :] = nodes_ref[...].astype(jnp.float32)

    def pick(p0, p1):
        return jnp.where(first_op, p0, p1)

    jac = [
        [[pick(jac_ref[d, u, 0, v], jac_ref[d, u, 1, v]) for v in range(VARS)] for u in range(VARS)]
        for d in range(3)
    ]
    damp = pick(damp_ref[0], damp_ref[1])
    freq = pick(freq_ref[0], freq_ref[1])

    for copy in coord_copies:
        copy.wait()

    for o in range(N_OP):
        for d in range(3):
            for h in range(2):
                nodebuf[d, 2 * o + h : 2 * o + h + 1, :] = cbuf[
                    o, d : d + 1, h * LANES : (h + 1) * LANES
                ]

    for tile in range(4):
        index = nodes_ref[:, tile * LANES : (tile + 1) * LANES]
        page = index // LANES
        within = lax.rem(index, LANES)
        for d in range(3):
            value = jnp.zeros((8, LANES), jnp.float32)
            for n in range(8):
                got = lanes_at(spread(nodebuf[d, n : n + 1, :]), within)
                value = jnp.where(page == n, got, value)
            stack[56 + 8 * d : 64 + 8 * d, tile * LANES : (tile + 1) * LANES] = value

    base = [jnp.floor(stack[56 + 8 * d : 57 + 8 * d, :] + 0.5).astype(jnp.int32) for d in range(3)]
    pos = base[0] * LANES + base[1] * 4 + base[2]
    onehot = (
        (lax.broadcasted_iota(jnp.int32, (CELLS_HERE, CELLS_HERE), 0) == pos)
        .astype(jnp.float32)
        .astype(jnp.bfloat16)
    )
    moved = move_cells(stack[...], onehot, 1)

    def to_lattice(array, rows, base_row):
        for j in range(STATE):
            row = base_row + 2 * j
            for l in range(4):
                lattice[array, j, 2 * l : 2 * l + 2, :] = rows[
                    row : row + 2, l * LANES : (l + 1) * LANES
                ]

    to_lattice(0, moved, 0)
    for l in range(4):
        for d in range(3):
            part = moved[56 + 8 * d : 64 + 8 * d, l * LANES : (l + 1) * LANES]
            corner_lat[d, :, 2 * l, :] = part
            corner_lat[d, :, 2 * l + 1, :] = part
        slot_lat[:, l, :] = moved[88:96, l * LANES : (l + 1) * LANES]

    def pos_of(cells):
        page = cells // LANES
        within = lax.rem(cells, LANES)
        value = jnp.zeros((8, LANES), jnp.int32)
        for n in range(4):
            got = lanes_at(spread(pos[:, n * LANES : (n + 1) * LANES]), within)
            value = jnp.where(page == n, got, value)
        return lax.rem(value, LANES)

    lower_map = pos_of(spread(send_ref[0:1, :]))
    upper_map = pos_of(spread(send_ref[1:2, :]))

    def pack(values, source):
        packed = []
        for g in range(GROUPS):
            total = values[4 * g]
            for r in range(1, 4):
                if 4 * g + r < STATE:
                    total = jnp.where(
                        layer == (source + r) % 4, pltpu.roll(values[4 * g + r], 2 * r, 0), total
                    )
            packed.append(total)
        return packed

    def exchange(number, up_from, low_to, down_from, high_to):
        up = pltpu.make_async_remote_copy(
            src_ref=up_from,
            dst_ref=low_to,
            send_sem=up_send_sem.at[number],
            recv_sem=up_recv_sem.at[number],
            device_id=(op, nxt),
            device_id_type=MESH,
        )
        down = pltpu.make_async_remote_copy(
            src_ref=down_from,
            dst_ref=high_to,
            send_sem=down_send_sem.at[number],
            recv_sem=down_recv_sem.at[number],
            device_id=(op, prv),
            device_id_type=MESH,
        )
        up.start()
        down.start()
        copies.extend((up, down))

    copies = []

    def end_names(side):
        tile = 3 * side
        row = moved[80 + side : 81 + side, tile * LANES : (tile + 1) * LANES]
        named = spread(row.astype(jnp.int32)) - CELLS_HERE - side * LANES
        return jnp.clip(named, 0, LANES - 1)

    low_names, high_names = end_names(0), end_names(1)
    map_up[0] = upper_map.astype(jnp.float32)
    map_up[1] = high_names.astype(jnp.float32)
    map_down[0] = lower_map.astype(jnp.float32)
    map_down[1] = low_names.astype(jnp.float32)
    exchange(0, lattice.at[0], low_state.at[0], lattice.at[0], high_state.at[0])
    exchange(1, corner_lat, low_corner, corner_lat, high_corner)
    exchange(2, map_up, map_low, map_down, map_high)
    moved_late = move_cells(stack_late[...], onehot, 1)
    to_lattice(1, moved_late, 0)
    exchange(3, lattice.at[1], low_state.at[1], lattice.at[1], high_state.at[1])
    to_lattice(2, moved_late, 50)
    flow = [lattice[2, j] for j in range(STATE)]
    for g, value in enumerate(pack(flow, 3)):
        up_send[g] = value
    for g, value in enumerate(pack(flow, 0)):
        down_send[g] = value
    exchange(4, up_send, low_recv, down_send, high_recv)

    inner = [None, None, lane >= 4, lane < LANES - 4, axial > 0, axial < 3]

    def geometry(points):
        corner = [[points[d, c] for d in range(3)] for c in range(8)]
        center = [sum(corner[c][d] for c in range(8)) * 0.125 for d in range(3)]
        normals, areas, offsets = [], [], []
        volume = jnp.zeros((8, LANES), jnp.float32)
        for c0, c1, c2, c3 in FACE_CORNERS:
            first = [corner[c2][d] - corner[c0][d] for d in range(3)]
            second = [corner[c3][d] - corner[c1][d] for d in range(3)]
            normal = [0.5 * x for x in cross(first, second)]
            offset = [
                0.25 * (corner[c0][d] + corner[c1][d] + corner[c2][d] + corner[c3][d]) - center[d]
                for d in range(3)
            ]
            volume = volume + sum(offset[d] * normal[d] for d in range(3))
            normals.append(normal)
            offsets.append(offset)
            areas.append(jnp.sqrt(sum(normal[d] * normal[d] for d in range(3))))
        volume = volume * (1.0 / 3.0)
        area_sum = sum(areas)
        normal_total = [sum(normals[k][d] for k in range(6)) for d in range(3)]
        step = COURANT / ((1.0 + damp) * area_sum + 2.0 * freq * volume)
        face_normal, face_area = [], []
        for k in range(6):
            keep = [0.5 * normals[k][d] for d in range(3)]
            area = 0.5 * damp * areas[k]
            if inner[k] is not None:
                keep = [jnp.where(inner[k], x, 0.0) for x in keep]
                area = jnp.where(inner[k], area, 0.0)
            face_normal.append(keep)
            face_area.append(area)
        half_total = [0.5 * normal_total[d] for d in range(3)]
        sweep_terms = (face_normal, face_area, half_total, 0.5 * damp * area_sum, freq * volume, step)
        return sweep_terms, (corner, normals, areas, offsets, normal_total)

    own_terms, (corner, normals, areas, offsets, normal_total) = geometry(corner_lat)
    spectral = spectral_values()

    def ghosts():
        low, high = [], []
        for g in range(GROUPS):
            from_low = lanes_at(low_recv[g], ghost_index[0])
            from_high = lanes_at(high_recv[g], ghost_index[1])
            for r in range(4):
                if 4 * g + r < STATE:
                    low.append(pltpu.roll(from_low, (2 - 2 * r) % 8, 0))
                    high.append(pltpu.roll(from_high, (6 - 2 * r) % 8, 0))
        return low, high

    def turn(values):
        return [
            [
                sum(jac[d][u][v] * values[t * VARS + u] for u in range(VARS))
                for t in range(INST)
                for v in range(VARS)
            ]
            for d in range(3)
        ]

    def outgoing(terms, k, turned, adjoint, j):
        face_normal, face_area = terms[:2]
        return (
            face_normal[k][0] * turned[0][j]
            + face_normal[k][1] * turned[1][j]
            + face_normal[k][2] * turned[2][j]
            - face_area[k] * adjoint[j]
        )

    def faces(terms, adjoint):
        turned = turn(adjoint)
        up = [pltpu.roll(outgoing(terms, 1, turned, adjoint, j), 2, 0) for j in range(STATE)]
        down = [pltpu.roll(outgoing(terms, 0, turned, adjoint, j), 6, 0) for j in range(STATE)]
        return turned, up, down

    def inside(terms, turned, adjoint, objective):
        _, _, half_total, self_area, freq_volume, _ = terms
        updates = []
        for j in range(STATE):
            t, v = j // VARS, j % VARS
            update = (
                half_total[0] * turned[0][j]
                + half_total[1] * turned[1][j]
                + half_total[2] * turned[2][j]
                + self_area * adjoint[j]
                + objective(j)
            )
            mix = None
            for other in range(INST):
                if other != t:
                    term = float(spectral[other, t]) * adjoint[other * VARS + v]
                    mix = term if mix is None else mix + term
            update = update + freq_volume * mix
            update = update + pltpu.roll(outgoing(terms, 3, turned, adjoint, j), 4, 1)
            update = update + pltpu.roll(outgoing(terms, 2, turned, adjoint, j), LANES - 4, 1)
            update = update + pltpu.roll(outgoing(terms, 5, turned, adjoint, j), 1, 1)
            update = update + pltpu.roll(outgoing(terms, 4, turned, adjoint, j), LANES - 1, 1)
            updates.append(update)
        return updates

    def advance(terms, adjoint, updates, near):
        return [adjoint[j] - terms[5] * (updates[j] + near(j)) for j in range(STATE)]

    own = [lattice[0, j] for j in range(STATE)]
    own_turned, own_up, own_down = faces(own_terms, own)
    own_part = inside(own_terms, own_turned, own, lambda j: lattice[1, j])
    for j in range(STATE):
        first_part[j] = own_part[j]

    for copy in copies[:6]:
        copy.wait()

    ghost_index = [
        lanes_at(map_low[0].astype(jnp.int32), low_names),
        lanes_at(map_high[0].astype(jnp.int32), high_names),
    ]
    from_low_index = lanes_at(lower_map, map_low[1].astype(jnp.int32))
    from_high_index = lanes_at(upper_map, map_high[1].astype(jnp.int32))
    low_terms, _ = geometry(low_corner)
    high_terms, _ = geometry(high_corner)
    low = [low_state[0, j] for j in range(STATE)]
    high = [high_state[0, j] for j in range(STATE)]
    for copy in copies[6:8]:
        copy.wait()

    for sweep in range(2):
        if sweep > 0:
            own_turned, own_up, own_down = faces(own_terms, own)
            own_part = inside(own_terms, own_turned, own, lambda j: lattice[1, j])
        else:
            own_part = [first_part[j] for j in range(STATE)]
        low_turned, low_up, low_down = faces(low_terms, low)
        low_part = inside(low_terms, low_turned, low, lambda j: low_state[1, j])
        low = advance(
            low_terms,
            low,
            low_part,
            lambda j: jnp.where(layer == 0, 0.0, low_up[j])
            + jnp.where(layer == 3, lanes_at(own_down[j], from_low_index), low_down[j]),
        )
        high_turned, high_up, high_down = faces(high_terms, high)
        high_part = inside(high_terms, high_turned, high, lambda j: high_state[1, j])
        high = advance(
            high_terms,
            high,
            high_part,
            lambda j: jnp.where(layer == 3, 0.0, high_down[j])
            + jnp.where(layer == 0, lanes_at(own_up[j], from_high_index), high_up[j]),
        )
        own = advance(
            own_terms,
            own,
            own_part,
            lambda j: jnp.where(layer == 0, lanes_at(low_up[j], ghost_index[0]), own_up[j])
            + jnp.where(layer == 3, lanes_at(high_down[j], ghost_index[1]), own_down[j]),
        )

    def halves(x, y):
        if isinstance(x, (tuple, list)):
            return [halves(a, b) for a, b in zip(x, y)]
        return jnp.where(layer >= 2, x, y)

    outer, outer_terms = halves(low, high), halves(low_terms, high_terms)
    for sweep in range(2, ITERS):
        own_turned, own_up, own_down = faces(own_terms, own)
        outer_turned, outer_up, outer_down = faces(outer_terms, outer)
        own_part = inside(own_terms, own_turned, own, lambda j: lattice[1, j])
        own = advance(
            own_terms,
            own,
            own_part,
            lambda j: jnp.where(layer == 0, lanes_at(outer_up[j], ghost_index[0]), own_up[j])
            + jnp.where(layer == 3, lanes_at(outer_down[j], ghost_index[1]), own_down[j]),
        )
        if sweep < ITERS - 1:
            outer_part = inside(
                outer_terms,
                outer_turned,
                outer,
                lambda j: halves(low_state[1, j], high_state[1, j]),
            )
            outer = advance(
                outer_terms,
                outer,
                outer_part,
                lambda j: jnp.where(layer == 0, lanes_at(own_up[j], from_high_index), outer_up[j])
                + jnp.where(layer == 3, lanes_at(own_down[j], from_low_index), outer_down[j]),
            )
    adjoint = own
    for copy in copies[8:]:
        copy.wait()

    low, high = ghosts()
    final_rows = turn(adjoint)
    along = [[None] * 3 for _ in range(6)]
    spread_sum = [None] * 6
    here = [None] * 3
    here_damp = None
    volume_sum = None

    def added(total, term):
        return term if total is None else total + term

    for t in range(INST):
        for v in range(VARS):
            j = t * VARS + v
            value = adjoint[j]
            own = lattice[2, j]
            final = [final_rows[d][j] for d in range(3)]
            mix = None
            for other in range(INST):
                if other != t:
                    mix = added(mix, float(spectral[t, other]) * lattice[2, other * VARS + v])
            volume_sum = added(volume_sum, value * mix)
            for d in range(3):
                here[d] = added(here[d], final[d] * own)
            here_damp = added(here_damp, value * own)
            far = [
                jnp.where(layer == 0, low[j], pltpu.roll(own, 2, 0)),
                jnp.where(layer == 3, high[j], pltpu.roll(own, 6, 0)),
                pltpu.roll(own, 4, 1),
                pltpu.roll(own, LANES - 4, 1),
                pltpu.roll(own, 1, 1),
                pltpu.roll(own, LANES - 1, 1),
            ]
            for k in range(6):
                for d in range(3):
                    along[k][d] = added(along[k][d], final[d] * far[k])
                spread_sum[k] = added(spread_sum[k], value * far[k])

    def both(x):
        return x + jnp.where(first_op, pltpu.roll(x, 7, 0), pltpu.roll(x, 1, 0))

    volume_grad = both(volume_sum * freq) * (WEIGHT / 3.0)
    cots = [[None] * 3 for _ in range(8)]
    center_cot = [-(0.125) * volume_grad * normal_total[d] for d in range(3)]
    for k, (c0, c1, c2, c3) in enumerate(FACE_CORNERS):
        far_along, far_damp = along[k], spread_sum[k]
        if inner[k] is not None:
            far_along = [jnp.where(inner[k], x, 0.0) for x in far_along]
            far_damp = jnp.where(inner[k], far_damp, 0.0)
        scale = both(damp * (here_damp - far_damp)) / areas[k]
        grad = [
            (0.5 * WEIGHT) * (both(here[d] + far_along[d]) + scale * normals[k][d])
            + volume_grad * offsets[k][d]
            for d in range(3)
        ]
        first = [corner[c2][d] - corner[c0][d] for d in range(3)]
        second = [corner[c3][d] - corner[c1][d] for d in range(3)]
        to_first = cross(second, grad)
        to_second = cross(grad, first)
        for d in range(3):
            middle = 0.25 * volume_grad * normals[k][d]
            cots[c0][d] = added(cots[c0][d], middle - 0.5 * to_first[d])
            cots[c2][d] = added(cots[c2][d], middle + 0.5 * to_first[d])
            cots[c1][d] = added(cots[c1][d], middle - 0.5 * to_second[d])
            cots[c3][d] = added(cots[c3][d], middle + 0.5 * to_second[d])
    cots = [[cots[c][d] + center_cot[d] for d in range(3)] for c in range(8)]

    def meet(bit, down, up, at_low, at_high):
        for c in range(8):
            if not c & bit:
                for d in range(3):
                    a, b = cots[c][d], cots[c | bit][d]
                    cots[c][d] = a + jnp.where(at_low, 0.0, down(b))
                    cots[c | bit][d] = b + jnp.where(at_high, 0.0, up(a))

    meet(1, lambda x: pltpu.roll(x, 1, 1), lambda x: pltpu.roll(x, LANES - 1, 1), axial == 0, axial == 3)
    meet(2, lambda x: pltpu.roll(x, 4, 1), lambda x: pltpu.roll(x, LANES - 4, 1), lane < 4, lane >= LANES - 4)
    meet(4, lambda x: pltpu.roll(x, 2, 0), lambda x: pltpu.roll(x, 6, 0), layer == 0, layer == 3)

    limits = (4, 32, 4)
    point = [
        jnp.clip(jnp.floor(jnp.clip(nodebuf[d], -1.0, 40.0) + 0.5).astype(jnp.int32), 0, limits[d])
        for d in range(3)
    ]
    home = [jnp.minimum(point[d], limits[d] - 1) for d in range(3)]
    source = ((point[0] - home[0]) * 4 + (point[1] - home[1]) * 2 + point[2] - home[2]) * 4 + home[0]
    within = home[1] * 4 + home[2]
    slot_number = sub * LANES + lane
    sens = [jnp.zeros((8, LANES), jnp.float32) for _ in range(3)]
    for c in range(8):
        slots = slot_lat[c]
        for l in range(4):
            name = lanes_at(spread(slots[l : l + 1]), within).astype(jnp.int32)
            chosen = jnp.logical_and(source == c * 4 + l, name == slot_number)
            for d in range(3):
                got = lanes_at(spread(cots[c][d][2 * l : 2 * l + 1]), within)
                sens[d] = jnp.where(chosen, got, sens[d])

    rs_send[...] = jnp.zeros_like(rs_send)
    for o in range(N_OP):
        for d in range(3):
            rs_send[o, 2 * d : 2 * d + 2, :] = sens[d][2 * o : 2 * o + 2]
    sums = []
    for j, peer in enumerate(peers):
        copy = pltpu.make_async_remote_copy(
            src_ref=rs_send.at[peer],
            dst_ref=rs_recv.at[j],
            send_sem=r_send_sem.at[j],
            recv_sem=r_recv_sem.at[j],
            device_id=(peer, cell),
            device_id_type=MESH,
        )
        copy.start()
        sums.append(copy)

    outbuf[48:56, :] = jnp.zeros((8, CELLS_HERE), jnp.float32)
    for j in range(STATE):
        for l in range(4):
            outbuf[2 * j : 2 * j + 2, l * LANES : (l + 1) * LANES] = adjoint[j][2 * l : 2 * l + 2]
    back = move_cells(outbuf[...], onehot, 0)
    for j in range(STATE):
        out_ref[j] = back[2 * j : 2 * j + 2]
    put = pltpu.make_async_copy(out_ref, out_hbm, out_sem)
    put.start()

    total = rs_send[op]
    for j, copy in enumerate(sums):
        copy.wait()
        total = total + rs_recv[j]
    for d in range(3):
        for h in range(2):
            sens_ref[d : d + 1, h * LANES : (h + 1) * LANES] = total[2 * d + h : 2 * d + h + 1]
    put.wait()


def per_device(
    flow_state,
    adjoint_start,
    objective_grad,
    adjacency,
    send_list,
    cell_nodes,
    coords,
    jacobians,
    dissipation,
    frequency,
):
    anywhere = pl.BlockSpec(memory_space=pl.ANY)
    f32, i32 = jnp.float32, jnp.int32
    dma = pltpu.SemaphoreType.DMA

    def pairs(x):
        return x.transpose(1, 2, 0, 3).reshape(STATE, OPS_HERE, CELLS_HERE)

    rows = pltpu.VMEM((STATE, OPS_HERE, CELLS_HERE), f32)
    message = pltpu.VMEM((GROUPS, 8, LANES), f32)
    maps = pltpu.VMEM((2, 8, LANES), f32)
    block = pltpu.VMEM((2, STATE, 8, LANES), f32)
    points = pltpu.VMEM((3, 8, 8, LANES), f32)
    adjoint, sens = pl.pallas_call(
        kernel,
        out_shape=(
            jax.ShapeDtypeStruct((STATE, OPS_HERE, CELLS_HERE), f32),
            jax.ShapeDtypeStruct(coords.shape, f32),
        ),
        in_specs=[anywhere] * 10,
        out_specs=(anywhere, pl.BlockSpec(memory_space=pltpu.VMEM)),
        scratch_shapes=[
            rows,
            rows,
            rows,
            pltpu.VMEM((6, CELLS_HERE), i32),
            pltpu.VMEM((2, LANES), i32),
            pltpu.VMEM((8, CELLS_HERE), i32),
            pltpu.VMEM((3, 256), f32),
            pltpu.SMEM((3, VARS, OPS_HERE, VARS), f32),
            pltpu.SMEM((OPS_HERE,), f32),
            pltpu.SMEM((OPS_HERE,), f32),
            rows,
            pltpu.VMEM((N_OP, 3, 256), f32),
            pltpu.VMEM((3, 8, LANES), f32),
            pltpu.VMEM((96, CELLS_HERE), f32),
            pltpu.VMEM((104, CELLS_HERE), f32),
            pltpu.VMEM((3, STATE, 8, LANES), f32),
            pltpu.VMEM((3, 8, 8, LANES), f32),
            pltpu.VMEM((8, 8, LANES), f32),
            message,
            message,
            message,
            message,
            maps,
            maps,
            maps,
            maps,
            block,
            block,
            points,
            points,
            pltpu.VMEM((STATE, 8, LANES), f32),
            pltpu.VMEM((N_OP, 8, LANES), f32),
            pltpu.VMEM((N_OP - 1, 8, LANES), f32),
            pltpu.VMEM((56, CELLS_HERE), f32),
            dma((10,)),
            dma,
            dma((3,)),
            dma((3,)),
            dma((3,)),
            dma((3,)),
            dma((5,)),
            dma((5,)),
            dma((5,)),
            dma((5,)),
        ],
        compiler_params=pltpu.CompilerParams(collective_id=0, has_side_effects=True),
    )(
        pairs(flow_state),
        pairs(adjoint_start),
        pairs(objective_grad),
        adjacency,
        send_list.reshape(2, LANES),
        cell_nodes,
        coords,
        jacobians.transpose(1, 2, 0, 3),
        dissipation,
        frequency,
    )
    adjoint = adjoint.reshape(INST, VARS, OPS_HERE, CELLS_HERE).transpose(2, 0, 1, 3)
    return adjoint, sens


def solution(mesh):
    in_specs = (
        P("op", None, None, "cell"),
        P("op", None, None, "cell"),
        P("op", None, None, "cell"),
        P(None, "cell"),
        P("cell"),
        P(None, "cell"),
        P(None, ("op", "cell")),
        P("op", None, None, None),
        P("op"),
        P("op"),
    )
    out_specs = (P("op", None, None, "cell"), P(None, ("op", "cell")))
    return jax.shard_map(
        per_device, mesh=mesh, in_specs=in_specs, out_specs=out_specs, check_vma=False
    )
```

```python
import functools
import math

import jax
import jax.numpy as jnp
import numpy as np
from jax import lax
from jax.experimental import pallas as pl
from jax.experimental.pallas import tpu as pltpu
from jax.sharding import PartitionSpec as P

ITERS = 4
INST = 5
VARS = 5
OPS_HERE = 2
N_OP = 4
LANES = 128
CELLS_HERE = 512
FACE_CORNERS = ((0, 1, 3, 2), (4, 6, 7, 5), (0, 4, 5, 1), (2, 3, 7, 6), (0, 2, 6, 4), (1, 5, 7, 3))
COURANT = 1.2
WEIGHT = 1.0 / 8
STATE = INST * VARS
GROUPS = (STATE + 3) // 4
MESH = pl.DeviceIdType.MESH


def spectral_values():
    values = np.zeros((INST, INST))
    for t in range(INST):
        for s in range(INST):
            if t != s:
                values[t, s] = 0.5 * (-1.0) ** (t - s) / math.sin(math.pi * (t - s) / INST)
    return values


def lanes_at(table, index):
    return jnp.take_along_axis(table, index, axis=1, mode="promise_in_bounds")


def split3(x):
    hi = x.astype(jnp.bfloat16)
    rest = x - hi.astype(jnp.float32)
    mid = rest.astype(jnp.bfloat16)
    low = (rest - mid.astype(jnp.float32)).astype(jnp.bfloat16)
    return jnp.concatenate([hi, mid, low], axis=0)


def move_cells(x, onehot, contract):
    rows = x.shape[0]
    y = lax.dot_general(
        split3(x), onehot, (((1,), (contract,)), ((), ())), preferred_element_type=jnp.float32
    )
    return y[:rows] + y[rows : 2 * rows] + y[2 * rows :]


def spread(row):
    return jnp.broadcast_to(row, (8, LANES))


def cross(a, b):
    return [a[1] * b[2] - a[2] * b[1], a[2] * b[0] - a[0] * b[2], a[0] * b[1] - a[1] * b[0]]


def kernel(
    state_in,
    start_in,
    objective_in,
    adjacency_in,
    send_in,
    nodes_in,
    coords_in,
    jac_in,
    damp_in,
    freq_in,
    out_hbm,
    sens_ref,
    state_ref,
    start_ref,
    objective_ref,
    adjacency_ref,
    send_ref,
    nodes_ref,
    coords_ref,
    jac_ref,
    damp_ref,
    freq_ref,
    out_ref,
    cbuf,
    nodebuf,
    stack,
    stack_late,
    lattice,
    corner_lat,
    slot_lat,
    up_send,
    down_send,
    low_recv,
    high_recv,
    map_up,
    map_down,
    map_low,
    map_high,
    low_state,
    high_state,
    low_corner,
    high_corner,
    first_part,
    corner_pack,
    low_pack,
    high_pack,
    rs_send,
    rs_recv,
    outbuf,
    fetch_sem,
    out_sem,
    c_send_sem,
    c_recv_sem,
    r_send_sem,
    r_recv_sem,
    up_send_sem,
    up_recv_sem,
    down_send_sem,
    down_recv_sem,
):
    op = lax.axis_index("op")
    cell = lax.axis_index("cell")
    n_cell = 128
    nxt = lax.rem(cell + 1, n_cell)
    prv = lax.rem(cell + n_cell - 1, n_cell)
    peers = [lax.rem(op + j, N_OP) for j in range(1, N_OP)]

    fetches = []
    pairs = (
        (coords_in, coords_ref),
        (nodes_in, nodes_ref),
        (adjacency_in, adjacency_ref),
        (send_in, send_ref),
        (start_in, start_ref),
        (jac_in, jac_ref),
        (damp_in, damp_ref),
        (freq_in, freq_ref),
        (objective_in, objective_ref),
        (state_in, state_ref),
    )
    for j, (source, target) in enumerate(pairs):
        fetch = pltpu.make_async_copy(source, target, fetch_sem.at[j])
        fetch.start()
        fetches.append(fetch)

    barrier = pltpu.get_barrier_semaphore()
    for peer in peers:
        pl.semaphore_signal(barrier, inc=1, device_id=(peer, cell), device_id_type=MESH)
    for block in (prv, nxt):
        pl.semaphore_signal(barrier, inc=1, device_id=(op, block), device_id_type=MESH)
    pl.semaphore_wait(barrier, 5)
    fetches[0].wait()

    coord_copies = []
    for j, peer in enumerate(peers):
        copy = pltpu.make_async_remote_copy(
            src_ref=coords_ref,
            dst_ref=cbuf.at[op],
            send_sem=c_send_sem.at[j],
            recv_sem=c_recv_sem.at[j],
            device_id=(peer, cell),
            device_id_type=MESH,
        )
        copy.start()
        coord_copies.append(copy)
    cbuf[op] = coords_ref[...]

    sub = lax.broadcasted_iota(jnp.int32, (8, LANES), 0)
    lane = lax.broadcasted_iota(jnp.int32, (8, LANES), 1)
    layer = sub // 2
    first_op = lax.rem(sub, 2) == 0
    axial = lax.rem(lane, 4)
    for fetch in fetches[1:]:
        fetch.wait()
    stack[48:56, :] = jnp.zeros((8, CELLS_HERE), jnp.float32)
    stack[80:88, :] = jnp.zeros((8, CELLS_HERE), jnp.float32)
    stack_late[96:104, :] = jnp.zeros((8, CELLS_HERE), jnp.float32)
    for j in range(STATE):
        stack[2 * j : 2 * j + 2, :] = start_ref[j]
        stack_late[2 * j : 2 * j + 2, :] = objective_ref[j]
        stack_late[50 + 2 * j : 52 + 2 * j, :] = state_ref[j]
    stack[80:86, :] = adjacency_ref[...].astype(jnp.float32)
    stack[88:96, :] = nodes_ref[...].astype(jnp.float32)

    def pick(p0, p1):
        return jnp.where(first_op, p0, p1)

    jac = [
        [[pick(jac_ref[d, u, 0, v], jac_ref[d, u, 1, v]) for v in range(VARS)] for u in range(VARS)]
        for d in range(3)
    ]
    damp = pick(damp_ref[0], damp_ref[1])
    freq = pick(freq_ref[0], freq_ref[1])

    for copy in coord_copies:
        copy.wait()

    for o in range(N_OP):
        for d in range(3):
            for h in range(2):
                nodebuf[d, 2 * o + h : 2 * o + h + 1, :] = cbuf[
                    o, d : d + 1, h * LANES : (h + 1) * LANES
                ]

    for tile in range(4):
        index = nodes_ref[:, tile * LANES : (tile + 1) * LANES]
        page = index // LANES
        within = lax.rem(index, LANES)
        for d in range(3):
            value = jnp.zeros((8, LANES), jnp.float32)
            for n in range(8):
                got = lanes_at(spread(nodebuf[d, n : n + 1, :]), within)
                value = jnp.where(page == n, got, value)
            stack[56 + 8 * d : 64 + 8 * d, tile * LANES : (tile + 1) * LANES] = value

    base = [jnp.floor(stack[56 + 8 * d : 57 + 8 * d, :] + 0.5).astype(jnp.int32) for d in range(3)]
    pos = base[0] * LANES + base[1] * 4 + base[2]
    onehot = (
        (lax.broadcasted_iota(jnp.int32, (CELLS_HERE, CELLS_HERE), 0) == pos)
        .astype(jnp.float32)
        .astype(jnp.bfloat16)
    )
    moved = move_cells(stack[...], onehot, 1)

    def to_lattice(array, rows, base_row):
        for j in range(STATE):
            row = base_row + 2 * j
            for l in range(4):
                lattice[array, j, 2 * l : 2 * l + 2, :] = rows[
                    row : row + 2, l * LANES : (l + 1) * LANES
                ]

    to_lattice(0, moved, 0)
    for l in range(4):
        for d in range(3):
            part = moved[56 + 8 * d : 64 + 8 * d, l * LANES : (l + 1) * LANES]
            corner_lat[d, :, 2 * l, :] = part
            corner_lat[d, :, 2 * l + 1, :] = part
            corner_pack[d, :, l, :] = part
        slot_lat[:, l, :] = moved[88:96, l * LANES : (l + 1) * LANES]

    def pos_of(cells):
        page = cells // LANES
        within = lax.rem(cells, LANES)
        value = jnp.zeros((8, LANES), jnp.int32)
        for n in range(4):
            got = lanes_at(spread(pos[:, n * LANES : (n + 1) * LANES]), within)
            value = jnp.where(page == n, got, value)
        return lax.rem(value, LANES)

    lower_map = pos_of(spread(send_ref[0:1, :]))
    upper_map = pos_of(spread(send_ref[1:2, :]))

    def pack(values, source):
        packed = []
        for g in range(GROUPS):
            total = values[4 * g]
            for r in range(1, 4):
                if 4 * g + r < STATE:
                    total = jnp.where(
                        layer == (source + r) % 4, pltpu.roll(values[4 * g + r], 2 * r, 0), total
                    )
            packed.append(total)
        return packed

    def exchange(number, up_from, low_to, down_from, high_to):
        up = pltpu.make_async_remote_copy(
            src_ref=up_from,
            dst_ref=low_to,
            send_sem=up_send_sem.at[number],
            recv_sem=up_recv_sem.at[number],
            device_id=(op, nxt),
            device_id_type=MESH,
        )
        down = pltpu.make_async_remote_copy(
            src_ref=down_from,
            dst_ref=high_to,
            send_sem=down_send_sem.at[number],
            recv_sem=down_recv_sem.at[number],
            device_id=(op, prv),
            device_id_type=MESH,
        )
        up.start()
        down.start()
        copies.extend((up, down))

    copies = []

    def end_names(side):
        tile = 3 * side
        row = moved[80 + side : 81 + side, tile * LANES : (tile + 1) * LANES]
        named = spread(row.astype(jnp.int32)) - CELLS_HERE - side * LANES
        return jnp.clip(named, 0, LANES - 1)

    low_names, high_names = end_names(0), end_names(1)
    map_up[0] = upper_map.astype(jnp.float32)
    map_up[1] = high_names.astype(jnp.float32)
    map_down[0] = lower_map.astype(jnp.float32)
    map_down[1] = low_names.astype(jnp.float32)
    exchange(0, corner_pack, low_pack, corner_pack, high_pack)
    exchange(1, map_up, map_low, map_down, map_high)
    exchange(2, lattice.at[0], low_state.at[0], lattice.at[0], high_state.at[0])
    moved_late = move_cells(stack_late[...], onehot, 1)
    to_lattice(1, moved_late, 0)
    exchange(3, lattice.at[1], low_state.at[1], lattice.at[1], high_state.at[1])
    to_lattice(2, moved_late, 50)
    flow = [lattice[2, j] for j in range(STATE)]
    for g, value in enumerate(pack(flow, 3)):
        up_send[g] = value
    for g, value in enumerate(pack(flow, 0)):
        down_send[g] = value
    exchange(4, up_send, low_recv, down_send, high_recv)

    inner = [None, None, lane >= 4, lane < LANES - 4, axial > 0, axial < 3]

    def geometry(points):
        corner = [[points[d, c] for d in range(3)] for c in range(8)]
        center = [sum(corner[c][d] for c in range(8)) * 0.125 for d in range(3)]
        normals, areas, offsets = [], [], []
        volume = jnp.zeros((8, LANES), jnp.float32)
        for c0, c1, c2, c3 in FACE_CORNERS:
            first = [corner[c2][d] - corner[c0][d] for d in range(3)]
            second = [corner[c3][d] - corner[c1][d] for d in range(3)]
            normal = [0.5 * x for x in cross(first, second)]
            offset = [
                0.25 * (corner[c0][d] + corner[c1][d] + corner[c2][d] + corner[c3][d]) - center[d]
                for d in range(3)
            ]
            volume = volume + sum(offset[d] * normal[d] for d in range(3))
            normals.append(normal)
            offsets.append(offset)
            areas.append(jnp.sqrt(sum(normal[d] * normal[d] for d in range(3))))
        volume = volume * (1.0 / 3.0)
        area_sum = sum(areas)
        normal_total = [sum(normals[k][d] for k in range(6)) for d in range(3)]
        step = COURANT / ((1.0 + damp) * area_sum + 2.0 * freq * volume)
        face_normal, face_area = [], []
        for k in range(6):
            keep = [0.5 * normals[k][d] for d in range(3)]
            area = 0.5 * damp * areas[k]
            if inner[k] is not None:
                keep = [jnp.where(inner[k], x, 0.0) for x in keep]
                area = jnp.where(inner[k], area, 0.0)
            face_normal.append(keep)
            face_area.append(area)
        half_total = [0.5 * normal_total[d] for d in range(3)]
        sweep_terms = (face_normal, face_area, half_total, 0.5 * damp * area_sum, freq * volume, step)
        return sweep_terms, (corner, normals, areas, offsets, normal_total)

    own_terms, (corner, normals, areas, offsets, normal_total) = geometry(corner_lat)
    spectral = spectral_values()

    def ghosts():
        low, high = [], []
        for g in range(GROUPS):
            from_low = lanes_at(low_recv[g], ghost_index[0])
            from_high = lanes_at(high_recv[g], ghost_index[1])
            for r in range(4):
                if 4 * g + r < STATE:
                    low.append(pltpu.roll(from_low, (2 - 2 * r) % 8, 0))
                    high.append(pltpu.roll(from_high, (6 - 2 * r) % 8, 0))
        return low, high

    def turn(values):
        return [
            [
                sum(jac[d][u][v] * values[t * VARS + u] for u in range(VARS))
                for t in range(INST)
                for v in range(VARS)
            ]
            for d in range(3)
        ]

    def outgoing(terms, k, turned, adjoint, j):
        face_normal, face_area = terms[:2]
        return (
            face_normal[k][0] * turned[0][j]
            + face_normal[k][1] * turned[1][j]
            + face_normal[k][2] * turned[2][j]
            - face_area[k] * adjoint[j]
        )

    def faces(terms, adjoint):
        turned = turn(adjoint)
        up = [pltpu.roll(outgoing(terms, 1, turned, adjoint, j), 2, 0) for j in range(STATE)]
        down = [pltpu.roll(outgoing(terms, 0, turned, adjoint, j), 6, 0) for j in range(STATE)]
        return turned, up, down

    def inside(terms, turned, adjoint, objective):
        _, _, half_total, self_area, freq_volume, _ = terms
        updates = []
        for j in range(STATE):
            t, v = j // VARS, j % VARS
            update = (
                half_total[0] * turned[0][j]
                + half_total[1] * turned[1][j]
                + half_total[2] * turned[2][j]
                + self_area * adjoint[j]
                + objective(j)
            )
            mix = None
            for other in range(INST):
                if other != t:
                    term = float(spectral[other, t]) * adjoint[other * VARS + v]
                    mix = term if mix is None else mix + term
            update = update + freq_volume * mix
            update = update + pltpu.roll(outgoing(terms, 3, turned, adjoint, j), 4, 1)
            update = update + pltpu.roll(outgoing(terms, 2, turned, adjoint, j), LANES - 4, 1)
            update = update + pltpu.roll(outgoing(terms, 5, turned, adjoint, j), 1, 1)
            update = update + pltpu.roll(outgoing(terms, 4, turned, adjoint, j), LANES - 1, 1)
            updates.append(update)
        return updates

    def advance(terms, adjoint, updates, near):
        return [adjoint[j] - terms[5] * (updates[j] + near(j)) for j in range(STATE)]

    own = [lattice[0, j] for j in range(STATE)]
    own_turned, own_up, own_down = faces(own_terms, own)
    own_part = inside(own_terms, own_turned, own, lambda j: lattice[1, j])
    for j in range(STATE):
        first_part[j] = own_part[j]

    limits = (4, 32, 4)
    point = [
        jnp.clip(jnp.floor(jnp.clip(nodebuf[d], -1.0, 40.0) + 0.5).astype(jnp.int32), 0, limits[d])
        for d in range(3)
    ]
    home = [jnp.minimum(point[d], limits[d] - 1) for d in range(3)]
    source = ((point[0] - home[0]) * 4 + (point[1] - home[1]) * 2 + point[2] - home[2]) * 4 + home[0]
    within = home[1] * 4 + home[2]
    slot_number = (sub * LANES + lane).astype(jnp.float32)
    name = jnp.full((8, LANES), -1.0, jnp.float32)
    for c in range(8):
        slots = slot_lat[c]
        for l in range(4):
            got = lanes_at(spread(slots[l : l + 1]), within)
            name = jnp.where(source == c * 4 + l, got, name)
    source = jnp.where(name == slot_number, source, -1)

    for copy in copies[:4]:
        copy.wait()
    for pack_ref, full_ref in ((low_pack, low_corner), (high_pack, high_corner)):
        for d in range(3):
            for l in range(4):
                part = pack_ref[d, :, l, :]
                full_ref[d, :, 2 * l, :] = part
                full_ref[d, :, 2 * l + 1, :] = part

    ghost_index = [
        lanes_at(map_low[0].astype(jnp.int32), low_names),
        lanes_at(map_high[0].astype(jnp.int32), high_names),
    ]
    from_low_index = lanes_at(lower_map, map_low[1].astype(jnp.int32))
    from_high_index = lanes_at(upper_map, map_high[1].astype(jnp.int32))
    low_terms, _ = geometry(low_corner)
    high_terms, _ = geometry(high_corner)
    for copy in copies[4:6]:
        copy.wait()
    low = [low_state[0, j] for j in range(STATE)]
    high = [high_state[0, j] for j in range(STATE)]
    for copy in copies[6:8]:
        copy.wait()

    for sweep in range(2):
        if sweep > 0:
            own_turned, own_up, own_down = faces(own_terms, own)
            own_part = inside(own_terms, own_turned, own, lambda j: lattice[1, j])
        else:
            own_part = [first_part[j] for j in range(STATE)]
        low_turned, low_up, low_down = faces(low_terms, low)
        low_part = inside(low_terms, low_turned, low, lambda j: low_state[1, j])
        low = advance(
            low_terms,
            low,
            low_part,
            lambda j: jnp.where(layer == 0, 0.0, low_up[j])
            + jnp.where(layer == 3, lanes_at(own_down[j], from_low_index), low_down[j]),
        )
        high_turned, high_up, high_down = faces(high_terms, high)
        high_part = inside(high_terms, high_turned, high, lambda j: high_state[1, j])
        high = advance(
            high_terms,
            high,
            high_part,
            lambda j: jnp.where(layer == 3, 0.0, high_down[j])
            + jnp.where(layer == 0, lanes_at(own_up[j], from_high_index), high_up[j]),
        )
        own = advance(
            own_terms,
            own,
            own_part,
            lambda j: jnp.where(layer == 0, lanes_at(low_up[j], ghost_index[0]), own_up[j])
            + jnp.where(layer == 3, lanes_at(high_down[j], ghost_index[1]), own_down[j]),
        )

    def halves(x, y):
        if isinstance(x, (tuple, list)):
            return [halves(a, b) for a, b in zip(x, y)]
        return jnp.where(layer >= 2, x, y)

    outer, outer_terms = halves(low, high), halves(low_terms, high_terms)
    for sweep in range(2, ITERS):
        own_turned, own_up, own_down = faces(own_terms, own)
        outer_turned, outer_up, outer_down = faces(outer_terms, outer)
        own_part = inside(own_terms, own_turned, own, lambda j: lattice[1, j])
        own = advance(
            own_terms,
            own,
            own_part,
            lambda j: jnp.where(layer == 0, lanes_at(outer_up[j], ghost_index[0]), own_up[j])
            + jnp.where(layer == 3, lanes_at(outer_down[j], ghost_index[1]), own_down[j]),
        )
        if sweep < ITERS - 1:
            outer_part = inside(
                outer_terms,
                outer_turned,
                outer,
                lambda j: halves(low_state[1, j], high_state[1, j]),
            )
            outer = advance(
                outer_terms,
                outer,
                outer_part,
                lambda j: jnp.where(layer == 0, lanes_at(own_up[j], from_high_index), outer_up[j])
                + jnp.where(layer == 3, lanes_at(own_down[j], from_low_index), outer_down[j]),
            )
    adjoint = own
    for copy in copies[8:]:
        copy.wait()

    low, high = ghosts()
    final_rows = turn(adjoint)
    along = [[None] * 3 for _ in range(6)]
    spread_sum = [None] * 6
    here = [None] * 3
    here_damp = None
    volume_sum = None

    def added(total, term):
        return term if total is None else total + term

    for t in range(INST):
        for v in range(VARS):
            j = t * VARS + v
            value = adjoint[j]
            own = lattice[2, j]
            final = [final_rows[d][j] for d in range(3)]
            mix = None
            for other in range(INST):
                if other != t:
                    mix = added(mix, float(spectral[t, other]) * lattice[2, other * VARS + v])
            volume_sum = added(volume_sum, value * mix)
            for d in range(3):
                here[d] = added(here[d], final[d] * own)
            here_damp = added(here_damp, value * own)
            far = [
                jnp.where(layer == 0, low[j], pltpu.roll(own, 2, 0)),
                jnp.where(layer == 3, high[j], pltpu.roll(own, 6, 0)),
                pltpu.roll(own, 4, 1),
                pltpu.roll(own, LANES - 4, 1),
                pltpu.roll(own, 1, 1),
                pltpu.roll(own, LANES - 1, 1),
            ]
            for k in range(6):
                for d in range(3):
                    along[k][d] = added(along[k][d], final[d] * far[k])
                spread_sum[k] = added(spread_sum[k], value * far[k])

    def both(x):
        return x + jnp.where(first_op, pltpu.roll(x, 7, 0), pltpu.roll(x, 1, 0))

    volume_grad = both(volume_sum * freq) * (WEIGHT / 3.0)
    cots = [[None] * 3 for _ in range(8)]
    center_cot = [-(0.125) * volume_grad * normal_total[d] for d in range(3)]
    for k, (c0, c1, c2, c3) in enumerate(FACE_CORNERS):
        far_along, far_damp = along[k], spread_sum[k]
        if inner[k] is not None:
            far_along = [jnp.where(inner[k], x, 0.0) for x in far_along]
            far_damp = jnp.where(inner[k], far_damp, 0.0)
        scale = both(damp * (here_damp - far_damp)) / areas[k]
        grad = [
            (0.5 * WEIGHT) * (both(here[d] + far_along[d]) + scale * normals[k][d])
            + volume_grad * offsets[k][d]
            for d in range(3)
        ]
        first = [corner[c2][d] - corner[c0][d] for d in range(3)]
        second = [corner[c3][d] - corner[c1][d] for d in range(3)]
        to_first = cross(second, grad)
        to_second = cross(grad, first)
        for d in range(3):
            middle = 0.25 * volume_grad * normals[k][d]
            cots[c0][d] = added(cots[c0][d], middle - 0.5 * to_first[d])
            cots[c2][d] = added(cots[c2][d], middle + 0.5 * to_first[d])
            cots[c1][d] = added(cots[c1][d], middle - 0.5 * to_second[d])
            cots[c3][d] = added(cots[c3][d], middle + 0.5 * to_second[d])
    cots = [[cots[c][d] + center_cot[d] for d in range(3)] for c in range(8)]

    def meet(bit, down, up, at_low, at_high):
        for c in range(8):
            if not c & bit:
                for d in range(3):
                    a, b = cots[c][d], cots[c | bit][d]
                    cots[c][d] = a + jnp.where(at_low, 0.0, down(b))
                    cots[c | bit][d] = b + jnp.where(at_high, 0.0, up(a))

    meet(1, lambda x: pltpu.roll(x, 1, 1), lambda x: pltpu.roll(x, LANES - 1, 1), axial == 0, axial == 3)
    meet(2, lambda x: pltpu.roll(x, 4, 1), lambda x: pltpu.roll(x, LANES - 4, 1), lane < 4, lane >= LANES - 4)
    meet(4, lambda x: pltpu.roll(x, 2, 0), lambda x: pltpu.roll(x, 6, 0), layer == 0, layer == 3)

    sens = [jnp.zeros((8, LANES), jnp.float32) for _ in range(3)]
    for c in range(8):
        for l in range(4):
            chosen = source == c * 4 + l
            for d in range(3):
                got = lanes_at(spread(cots[c][d][2 * l : 2 * l + 1]), within)
                sens[d] = jnp.where(chosen, got, sens[d])

    rs_send[...] = jnp.zeros_like(rs_send)
    for o in range(N_OP):
        for d in range(3):
            rs_send[o, 2 * d : 2 * d + 2, :] = sens[d][2 * o : 2 * o + 2]
    sums = []
    for j, peer in enumerate(peers):
        copy = pltpu.make_async_remote_copy(
            src_ref=rs_send.at[peer],
            dst_ref=rs_recv.at[j],
            send_sem=r_send_sem.at[j],
            recv_sem=r_recv_sem.at[j],
            device_id=(peer, cell),
            device_id_type=MESH,
        )
        copy.start()
        sums.append(copy)

    outbuf[48:56, :] = jnp.zeros((8, CELLS_HERE), jnp.float32)
    for j in range(STATE):
        for l in range(4):
            outbuf[2 * j : 2 * j + 2, l * LANES : (l + 1) * LANES] = adjoint[j][2 * l : 2 * l + 2]
    back = move_cells(outbuf[...], onehot, 0)
    for j in range(STATE):
        out_ref[j] = back[2 * j : 2 * j + 2]
    put = pltpu.make_async_copy(out_ref, out_hbm, out_sem)
    put.start()

    total = rs_send[op]
    for j, copy in enumerate(sums):
        copy.wait()
        total = total + rs_recv[j]
    for d in range(3):
        for h in range(2):
            sens_ref[d : d + 1, h * LANES : (h + 1) * LANES] = total[2 * d + h : 2 * d + h + 1]
    put.wait()


def per_device(
    flow_state,
    adjoint_start,
    objective_grad,
    adjacency,
    send_list,
    cell_nodes,
    coords,
    jacobians,
    dissipation,
    frequency,
):
    anywhere = pl.BlockSpec(memory_space=pl.ANY)
    f32, i32 = jnp.float32, jnp.int32
    dma = pltpu.SemaphoreType.DMA

    def pairs(x):
        return x.transpose(1, 2, 0, 3).reshape(STATE, OPS_HERE, CELLS_HERE)

    rows = pltpu.VMEM((STATE, OPS_HERE, CELLS_HERE), f32)
    message = pltpu.VMEM((GROUPS, 8, LANES), f32)
    maps = pltpu.VMEM((2, 8, LANES), f32)
    block = pltpu.VMEM((2, STATE, 8, LANES), f32)
    points = pltpu.VMEM((3, 8, 8, LANES), f32)
    packed = pltpu.VMEM((3, 8, 4, LANES), f32)
    adjoint, sens = pl.pallas_call(
        kernel,
        out_shape=(
            jax.ShapeDtypeStruct((STATE, OPS_HERE, CELLS_HERE), f32),
            jax.ShapeDtypeStruct(coords.shape, f32),
        ),
        in_specs=[anywhere] * 10,
        out_specs=(anywhere, pl.BlockSpec(memory_space=pltpu.VMEM)),
        scratch_shapes=[
            rows,
            rows,
            rows,
            pltpu.VMEM((6, CELLS_HERE), i32),
            pltpu.VMEM((2, LANES), i32),
            pltpu.VMEM((8, CELLS_HERE), i32),
            pltpu.VMEM((3, 256), f32),
            pltpu.SMEM((3, VARS, OPS_HERE, VARS), f32),
            pltpu.SMEM((OPS_HERE,), f32),
            pltpu.SMEM((OPS_HERE,), f32),
            rows,
            pltpu.VMEM((N_OP, 3, 256), f32),
            pltpu.VMEM((3, 8, LANES), f32),
            pltpu.VMEM((96, CELLS_HERE), f32),
            pltpu.VMEM((104, CELLS_HERE), f32),
            pltpu.VMEM((3, STATE, 8, LANES), f32),
            pltpu.VMEM((3, 8, 8, LANES), f32),
            pltpu.VMEM((8, 8, LANES), f32),
            message,
            message,
            message,
            message,
            maps,
            maps,
            maps,
            maps,
            block,
            block,
            points,
            points,
            pltpu.VMEM((STATE, 8, LANES), f32),
            packed,
            packed,
            packed,
            pltpu.VMEM((N_OP, 8, LANES), f32),
            pltpu.VMEM((N_OP - 1, 8, LANES), f32),
            pltpu.VMEM((56, CELLS_HERE), f32),
            dma((10,)),
            dma,
            dma((3,)),
            dma((3,)),
            dma((3,)),
            dma((3,)),
            dma((5,)),
            dma((5,)),
            dma((5,)),
            dma((5,)),
        ],
        compiler_params=pltpu.CompilerParams(collective_id=0, has_side_effects=True),
    )(
        pairs(flow_state),
        pairs(adjoint_start),
        pairs(objective_grad),
        adjacency,
        send_list.reshape(2, LANES),
        cell_nodes,
        coords,
        jacobians.transpose(1, 2, 0, 3),
        dissipation,
        frequency,
    )
    adjoint = adjoint.reshape(INST, VARS, OPS_HERE, CELLS_HERE).transpose(2, 0, 1, 3)
    return adjoint, sens


def solution(mesh):
    in_specs = (
        P("op", None, None, "cell"),
        P("op", None, None, "cell"),
        P("op", None, None, "cell"),
        P(None, "cell"),
        P("cell"),
        P(None, "cell"),
        P(None, ("op", "cell")),
        P("op", None, None, None),
        P("op"),
        P("op"),
    )
    out_specs = (P("op", None, None, "cell"), P(None, ("op", "cell")))
    return jax.shard_map(
        per_device, mesh=mesh, in_specs=in_specs, out_specs=out_specs, check_vma=False
    )
```

```python
import functools
import math

import jax
import jax.numpy as jnp
import numpy as np
from jax import lax
from jax.experimental import pallas as pl
from jax.experimental.pallas import tpu as pltpu
from jax.sharding import PartitionSpec as P

ITERS = 4
INST = 5
VARS = 5
OPS_HERE = 2
N_OP = 4
LANES = 128
CELLS_HERE = 512
FACE_CORNERS = ((0, 1, 3, 2), (4, 6, 7, 5), (0, 4, 5, 1), (2, 3, 7, 6), (0, 2, 6, 4), (1, 5, 7, 3))
COURANT = 1.2
WEIGHT = 1.0 / 8
STATE = INST * VARS
GROUPS = (STATE + 3) // 4
MESH = pl.DeviceIdType.MESH


def spectral_values():
    values = np.zeros((INST, INST))
    for t in range(INST):
        for s in range(INST):
            if t != s:
                values[t, s] = 0.5 * (-1.0) ** (t - s) / math.sin(math.pi * (t - s) / INST)
    return values


def lanes_at(table, index):
    return jnp.take_along_axis(table, index, axis=1, mode="promise_in_bounds")


def split3(x):
    hi = x.astype(jnp.bfloat16)
    rest = x - hi.astype(jnp.float32)
    mid = rest.astype(jnp.bfloat16)
    low = (rest - mid.astype(jnp.float32)).astype(jnp.bfloat16)
    return jnp.concatenate([hi, mid, low], axis=0)


def move_cells(x, onehot, contract):
    rows = x.shape[0]
    y = lax.dot_general(
        split3(x), onehot, (((1,), (contract,)), ((), ())), preferred_element_type=jnp.float32
    )
    return y[:rows] + y[rows : 2 * rows] + y[2 * rows :]


def spread(row):
    return jnp.broadcast_to(row, (8, LANES))


def cross(a, b):
    return [a[1] * b[2] - a[2] * b[1], a[2] * b[0] - a[0] * b[2], a[0] * b[1] - a[1] * b[0]]


def kernel(
    state_in,
    start_in,
    objective_in,
    adjacency_in,
    send_in,
    nodes_in,
    coords_in,
    jac_in,
    damp_in,
    freq_in,
    out_hbm,
    sens_ref,
    state_ref,
    start_ref,
    objective_ref,
    adjacency_ref,
    send_ref,
    nodes_ref,
    coords_ref,
    jac_ref,
    damp_ref,
    freq_ref,
    out_ref,
    cbuf,
    nodebuf,
    stack,
    stack_late,
    lattice,
    corner_lat,
    slot_lat,
    up_send,
    down_send,
    low_recv,
    high_recv,
    map_up,
    map_down,
    map_low,
    map_high,
    low_state,
    high_state,
    low_corner,
    high_corner,
    first_part,
    corner_pack,
    low_pack,
    high_pack,
    rs_send,
    rs_recv,
    outbuf,
    fetch_sem,
    out_sem,
    c_send_sem,
    c_recv_sem,
    r_send_sem,
    r_recv_sem,
    up_send_sem,
    up_recv_sem,
    down_send_sem,
    down_recv_sem,
):
    op = lax.axis_index("op")
    cell = lax.axis_index("cell")
    n_cell = 128
    nxt = lax.rem(cell + 1, n_cell)
    prv = lax.rem(cell + n_cell - 1, n_cell)
    peers = [lax.rem(op + j, N_OP) for j in range(1, N_OP)]

    fetches = []
    pairs = (
        (coords_in, coords_ref),
        (nodes_in, nodes_ref),
        (adjacency_in, adjacency_ref),
        (send_in, send_ref),
        (start_in, start_ref),
        (jac_in, jac_ref),
        (damp_in, damp_ref),
        (freq_in, freq_ref),
        (objective_in, objective_ref),
        (state_in, state_ref),
    )
    for j, (source, target) in enumerate(pairs):
        fetch = pltpu.make_async_copy(source, target, fetch_sem.at[j])
        fetch.start()
        fetches.append(fetch)

    barrier = pltpu.get_barrier_semaphore()
    for peer in peers:
        pl.semaphore_signal(barrier, inc=1, device_id=(peer, cell), device_id_type=MESH)
    for block in (prv, nxt):
        pl.semaphore_signal(barrier, inc=1, device_id=(op, block), device_id_type=MESH)
    pl.semaphore_wait(barrier, 5)
    fetches[0].wait()

    coord_copies = []
    for j, peer in enumerate(peers):
        copy = pltpu.make_async_remote_copy(
            src_ref=coords_ref,
            dst_ref=cbuf.at[op],
            send_sem=c_send_sem.at[j],
            recv_sem=c_recv_sem.at[j],
            device_id=(peer, cell),
            device_id_type=MESH,
        )
        copy.start()
        coord_copies.append(copy)
    cbuf[op] = coords_ref[...]

    sub = lax.broadcasted_iota(jnp.int32, (8, LANES), 0)
    lane = lax.broadcasted_iota(jnp.int32, (8, LANES), 1)
    layer = sub // 2
    first_op = lax.rem(sub, 2) == 0
    axial = lax.rem(lane, 4)
    for fetch in fetches[1:]:
        fetch.wait()
    stack[48:56, :] = jnp.zeros((8, CELLS_HERE), jnp.float32)
    stack[80:88, :] = jnp.zeros((8, CELLS_HERE), jnp.float32)
    stack_late[96:104, :] = jnp.zeros((8, CELLS_HERE), jnp.float32)
    for j in range(STATE):
        stack[2 * j : 2 * j + 2, :] = start_ref[j]
        stack_late[2 * j : 2 * j + 2, :] = objective_ref[j]
        stack_late[50 + 2 * j : 52 + 2 * j, :] = state_ref[j]
    stack[80:86, :] = adjacency_ref[...].astype(jnp.float32)
    stack[88:96, :] = nodes_ref[...].astype(jnp.float32)

    def pick(p0, p1):
        return jnp.where(first_op, p0, p1)

    jac = [
        [[pick(jac_ref[d, u, 0, v], jac_ref[d, u, 1, v]) for v in range(VARS)] for u in range(VARS)]
        for d in range(3)
    ]
    damp = pick(damp_ref[0], damp_ref[1])
    freq = pick(freq_ref[0], freq_ref[1])

    for copy in coord_copies:
        copy.wait_recv()

    for o in range(N_OP):
        for d in range(3):
            for h in range(2):
                nodebuf[d, 2 * o + h : 2 * o + h + 1, :] = cbuf[
                    o, d : d + 1, h * LANES : (h + 1) * LANES
                ]

    for tile in range(4):
        index = nodes_ref[:, tile * LANES : (tile + 1) * LANES]
        page = index // LANES
        within = lax.rem(index, LANES)
        for d in range(3):
            value = jnp.zeros((8, LANES), jnp.float32)
            for n in range(8):
                got = lanes_at(spread(nodebuf[d, n : n + 1, :]), within)
                value = jnp.where(page == n, got, value)
            stack[56 + 8 * d : 64 + 8 * d, tile * LANES : (tile + 1) * LANES] = value

    base = [jnp.floor(stack[56 + 8 * d : 57 + 8 * d, :] + 0.5).astype(jnp.int32) for d in range(3)]
    pos = base[0] * LANES + base[1] * 4 + base[2]
    onehot = (
        (lax.broadcasted_iota(jnp.int32, (CELLS_HERE, CELLS_HERE), 0) == pos)
        .astype(jnp.float32)
        .astype(jnp.bfloat16)
    )
    moved = move_cells(stack[...], onehot, 1)

    def to_lattice(array, rows, base_row):
        for j in range(STATE):
            row = base_row + 2 * j
            for l in range(4):
                lattice[array, j, 2 * l : 2 * l + 2, :] = rows[
                    row : row + 2, l * LANES : (l + 1) * LANES
                ]

    to_lattice(0, moved, 0)
    for l in range(4):
        for d in range(3):
            part = moved[56 + 8 * d : 64 + 8 * d, l * LANES : (l + 1) * LANES]
            corner_lat[d, :, 2 * l, :] = part
            corner_lat[d, :, 2 * l + 1, :] = part
            corner_pack[d, :, l, :] = part
        slot_lat[:, l, :] = moved[88:96, l * LANES : (l + 1) * LANES]

    def pos_of(cells):
        page = cells // LANES
        within = lax.rem(cells, LANES)
        value = jnp.zeros((8, LANES), jnp.int32)
        for n in range(4):
            got = lanes_at(spread(pos[:, n * LANES : (n + 1) * LANES]), within)
            value = jnp.where(page == n, got, value)
        return lax.rem(value, LANES)

    lower_map = pos_of(spread(send_ref[0:1, :]))
    upper_map = pos_of(spread(send_ref[1:2, :]))

    def pack(values, source):
        packed = []
        for g in range(GROUPS):
            total = values[4 * g]
            for r in range(1, 4):
                if 4 * g + r < STATE:
                    total = jnp.where(
                        layer == (source + r) % 4, pltpu.roll(values[4 * g + r], 2 * r, 0), total
                    )
            packed.append(total)
        return packed

    def exchange(number, up_from, low_to, down_from, high_to):
        up = pltpu.make_async_remote_copy(
            src_ref=up_from,
            dst_ref=low_to,
            send_sem=up_send_sem.at[number],
            recv_sem=up_recv_sem.at[number],
            device_id=(op, nxt),
            device_id_type=MESH,
        )
        down = pltpu.make_async_remote_copy(
            src_ref=down_from,
            dst_ref=high_to,
            send_sem=down_send_sem.at[number],
            recv_sem=down_recv_sem.at[number],
            device_id=(op, prv),
            device_id_type=MESH,
        )
        up.start()
        down.start()
        copies.extend((up, down))

    copies = []

    def end_names(side):
        tile = 3 * side
        row = moved[80 + side : 81 + side, tile * LANES : (tile + 1) * LANES]
        named = spread(row.astype(jnp.int32)) - CELLS_HERE - side * LANES
        return jnp.clip(named, 0, LANES - 1)

    low_names, high_names = end_names(0), end_names(1)
    map_up[0] = upper_map.astype(jnp.float32)
    map_up[1] = high_names.astype(jnp.float32)
    map_down[0] = lower_map.astype(jnp.float32)
    map_down[1] = low_names.astype(jnp.float32)
    exchange(0, corner_pack, low_pack, corner_pack, high_pack)
    exchange(1, map_up, map_low, map_down, map_high)
    exchange(2, lattice.at[0], low_state.at[0], lattice.at[0], high_state.at[0])
    moved_late = move_cells(stack_late[...], onehot, 1)
    to_lattice(1, moved_late, 0)
    exchange(3, lattice.at[1], low_state.at[1], lattice.at[1], high_state.at[1])
    to_lattice(2, moved_late, 50)
    flow = [lattice[2, j] for j in range(STATE)]
    for g, value in enumerate(pack(flow, 3)):
        up_send[g] = value
    for g, value in enumerate(pack(flow, 0)):
        down_send[g] = value
    exchange(4, up_send, low_recv, down_send, high_recv)

    inner = [None, None, lane >= 4, lane < LANES - 4, axial > 0, axial < 3]

    def geometry(points):
        corner = [[points[d, c] for d in range(3)] for c in range(8)]
        center = [sum(corner[c][d] for c in range(8)) * 0.125 for d in range(3)]
        normals, areas, offsets = [], [], []
        volume = jnp.zeros((8, LANES), jnp.float32)
        for c0, c1, c2, c3 in FACE_CORNERS:
            first = [corner[c2][d] - corner[c0][d] for d in range(3)]
            second = [corner[c3][d] - corner[c1][d] for d in range(3)]
            normal = [0.5 * x for x in cross(first, second)]
            offset = [
                0.25 * (corner[c0][d] + corner[c1][d] + corner[c2][d] + corner[c3][d]) - center[d]
                for d in range(3)
            ]
            volume = volume + sum(offset[d] * normal[d] for d in range(3))
            normals.append(normal)
            offsets.append(offset)
            areas.append(jnp.sqrt(sum(normal[d] * normal[d] for d in range(3))))
        volume = volume * (1.0 / 3.0)
        area_sum = sum(areas)
        normal_total = [sum(normals[k][d] for k in range(6)) for d in range(3)]
        step = COURANT / ((1.0 + damp) * area_sum + 2.0 * freq * volume)
        face_normal, face_area = [], []
        for k in range(6):
            keep = [0.5 * normals[k][d] for d in range(3)]
            area = 0.5 * damp * areas[k]
            if inner[k] is not None:
                keep = [jnp.where(inner[k], x, 0.0) for x in keep]
                area = jnp.where(inner[k], area, 0.0)
            face_normal.append(keep)
            face_area.append(area)
        half_total = [0.5 * normal_total[d] for d in range(3)]
        sweep_terms = (face_normal, face_area, half_total, 0.5 * damp * area_sum, freq * volume, step)
        return sweep_terms, (corner, normals, areas, offsets, normal_total)

    own_terms, (corner, normals, areas, offsets, normal_total) = geometry(corner_lat)
    spectral = spectral_values()

    def ghosts():
        low, high = [], []
        for g in range(GROUPS):
            from_low = lanes_at(low_recv[g], ghost_index[0])
            from_high = lanes_at(high_recv[g], ghost_index[1])
            for r in range(4):
                if 4 * g + r < STATE:
                    low.append(pltpu.roll(from_low, (2 - 2 * r) % 8, 0))
                    high.append(pltpu.roll(from_high, (6 - 2 * r) % 8, 0))
        return low, high

    def turn(values):
        return [
            [
                sum(jac[d][u][v] * values[t * VARS + u] for u in range(VARS))
                for t in range(INST)
                for v in range(VARS)
            ]
            for d in range(3)
        ]

    def outgoing(terms, k, turned, adjoint, j):
        face_normal, face_area = terms[:2]
        return (
            face_normal[k][0] * turned[0][j]
            + face_normal[k][1] * turned[1][j]
            + face_normal[k][2] * turned[2][j]
            - face_area[k] * adjoint[j]
        )

    def faces(terms, adjoint):
        turned = turn(adjoint)
        up = [pltpu.roll(outgoing(terms, 1, turned, adjoint, j), 2, 0) for j in range(STATE)]
        down = [pltpu.roll(outgoing(terms, 0, turned, adjoint, j), 6, 0) for j in range(STATE)]
        return turned, up, down

    def inside(terms, turned, adjoint, objective):
        _, _, half_total, self_area, freq_volume, _ = terms
        updates = []
        for j in range(STATE):
            t, v = j // VARS, j % VARS
            update = (
                half_total[0] * turned[0][j]
                + half_total[1] * turned[1][j]
                + half_total[2] * turned[2][j]
                + self_area * adjoint[j]
                + objective(j)
            )
            mix = None
            for other in range(INST):
                if other != t:
                    term = float(spectral[other, t]) * adjoint[other * VARS + v]
                    mix = term if mix is None else mix + term
            update = update + freq_volume * mix
            update = update + pltpu.roll(outgoing(terms, 3, turned, adjoint, j), 4, 1)
            update = update + pltpu.roll(outgoing(terms, 2, turned, adjoint, j), LANES - 4, 1)
            update = update + pltpu.roll(outgoing(terms, 5, turned, adjoint, j), 1, 1)
            update = update + pltpu.roll(outgoing(terms, 4, turned, adjoint, j), LANES - 1, 1)
            updates.append(update)
        return updates

    def advance(terms, adjoint, updates, near):
        return [adjoint[j] - terms[5] * (updates[j] + near(j)) for j in range(STATE)]

    own = [lattice[0, j] for j in range(STATE)]
    own_turned, own_up, own_down = faces(own_terms, own)
    own_part = inside(own_terms, own_turned, own, lambda j: lattice[1, j])
    for j in range(STATE):
        first_part[j] = own_part[j]

    limits = (4, 32, 4)
    point = [
        jnp.clip(jnp.floor(jnp.clip(nodebuf[d], -1.0, 40.0) + 0.5).astype(jnp.int32), 0, limits[d])
        for d in range(3)
    ]
    home = [jnp.minimum(point[d], limits[d] - 1) for d in range(3)]
    source = ((point[0] - home[0]) * 4 + (point[1] - home[1]) * 2 + point[2] - home[2]) * 4 + home[0]
    within = home[1] * 4 + home[2]
    slot_number = (sub * LANES + lane).astype(jnp.float32)
    name = jnp.full((8, LANES), -1.0, jnp.float32)
    for c in range(8):
        slots = slot_lat[c]
        for l in range(4):
            got = lanes_at(spread(slots[l : l + 1]), within)
            name = jnp.where(source == c * 4 + l, got, name)
    source = jnp.where(name == slot_number, source, -1)

    for copy in copies[:4]:
        copy.wait_recv()
    for pack_ref, full_ref in ((low_pack, low_corner), (high_pack, high_corner)):
        for d in range(3):
            for l in range(4):
                part = pack_ref[d, :, l, :]
                full_ref[d, :, 2 * l, :] = part
                full_ref[d, :, 2 * l + 1, :] = part

    ghost_index = [
        lanes_at(map_low[0].astype(jnp.int32), low_names),
        lanes_at(map_high[0].astype(jnp.int32), high_names),
    ]
    from_low_index = lanes_at(lower_map, map_low[1].astype(jnp.int32))
    from_high_index = lanes_at(upper_map, map_high[1].astype(jnp.int32))
    low_terms, _ = geometry(low_corner)
    high_terms, _ = geometry(high_corner)
    for copy in copies[4:6]:
        copy.wait_recv()
    low = [low_state[0, j] for j in range(STATE)]
    high = [high_state[0, j] for j in range(STATE)]
    for copy in copies[6:8]:
        copy.wait_recv()

    for sweep in range(2):
        if sweep > 0:
            own_turned, own_up, own_down = faces(own_terms, own)
            own_part = inside(own_terms, own_turned, own, lambda j: lattice[1, j])
        else:
            own_part = [first_part[j] for j in range(STATE)]
        low_turned, low_up, low_down = faces(low_terms, low)
        low_part = inside(low_terms, low_turned, low, lambda j: low_state[1, j])
        low = advance(
            low_terms,
            low,
            low_part,
            lambda j: jnp.where(layer == 0, 0.0, low_up[j])
            + jnp.where(layer == 3, lanes_at(own_down[j], from_low_index), low_down[j]),
        )
        high_turned, high_up, high_down = faces(high_terms, high)
        high_part = inside(high_terms, high_turned, high, lambda j: high_state[1, j])
        high = advance(
            high_terms,
            high,
            high_part,
            lambda j: jnp.where(layer == 3, 0.0, high_down[j])
            + jnp.where(layer == 0, lanes_at(own_up[j], from_high_index), high_up[j]),
        )
        own = advance(
            own_terms,
            own,
            own_part,
            lambda j: jnp.where(layer == 0, lanes_at(low_up[j], ghost_index[0]), own_up[j])
            + jnp.where(layer == 3, lanes_at(high_down[j], ghost_index[1]), own_down[j]),
        )

    def halves(x, y):
        if isinstance(x, (tuple, list)):
            return [halves(a, b) for a, b in zip(x, y)]
        return jnp.where(layer >= 2, x, y)

    outer, outer_terms = halves(low, high), halves(low_terms, high_terms)
    for sweep in range(2, ITERS):
        own_turned, own_up, own_down = faces(own_terms, own)
        outer_turned, outer_up, outer_down = faces(outer_terms, outer)
        own_part = inside(own_terms, own_turned, own, lambda j: lattice[1, j])
        own = advance(
            own_terms,
            own,
            own_part,
            lambda j: jnp.where(layer == 0, lanes_at(outer_up[j], ghost_index[0]), own_up[j])
            + jnp.where(layer == 3, lanes_at(outer_down[j], ghost_index[1]), own_down[j]),
        )
        if sweep < ITERS - 1:
            outer_part = inside(
                outer_terms,
                outer_turned,
                outer,
                lambda j: halves(low_state[1, j], high_state[1, j]),
            )
            outer = advance(
                outer_terms,
                outer,
                outer_part,
                lambda j: jnp.where(layer == 0, lanes_at(own_up[j], from_high_index), outer_up[j])
                + jnp.where(layer == 3, lanes_at(own_down[j], from_low_index), outer_down[j]),
            )
    adjoint = own
    for copy in copies[8:]:
        copy.wait_recv()

    low, high = ghosts()
    final_rows = turn(adjoint)
    along = [[None] * 3 for _ in range(6)]
    spread_sum = [None] * 6
    here = [None] * 3
    here_damp = None
    volume_sum = None

    def added(total, term):
        return term if total is None else total + term

    for t in range(INST):
        for v in range(VARS):
            j = t * VARS + v
            value = adjoint[j]
            own = lattice[2, j]
            final = [final_rows[d][j] for d in range(3)]
            mix = None
            for other in range(INST):
                if other != t:
                    mix = added(mix, float(spectral[t, other]) * lattice[2, other * VARS + v])
            volume_sum = added(volume_sum, value * mix)
            for d in range(3):
                here[d] = added(here[d], final[d] * own)
            here_damp = added(here_damp, value * own)
            far = [
                jnp.where(layer == 0, low[j], pltpu.roll(own, 2, 0)),
                jnp.where(layer == 3, high[j], pltpu.roll(own, 6, 0)),
                pltpu.roll(own, 4, 1),
                pltpu.roll(own, LANES - 4, 1),
                pltpu.roll(own, 1, 1),
                pltpu.roll(own, LANES - 1, 1),
            ]
            for k in range(6):
                for d in range(3):
                    along[k][d] = added(along[k][d], final[d] * far[k])
                spread_sum[k] = added(spread_sum[k], value * far[k])

    def both(x):
        return x + jnp.where(first_op, pltpu.roll(x, 7, 0), pltpu.roll(x, 1, 0))

    volume_grad = both(volume_sum * freq) * (WEIGHT / 3.0)
    cots = [[None] * 3 for _ in range(8)]
    center_cot = [-(0.125) * volume_grad * normal_total[d] for d in range(3)]
    for k, (c0, c1, c2, c3) in enumerate(FACE_CORNERS):
        far_along, far_damp = along[k], spread_sum[k]
        if inner[k] is not None:
            far_along = [jnp.where(inner[k], x, 0.0) for x in far_along]
            far_damp = jnp.where(inner[k], far_damp, 0.0)
        scale = both(damp * (here_damp - far_damp)) / areas[k]
        grad = [
            (0.5 * WEIGHT) * (both(here[d] + far_along[d]) + scale * normals[k][d])
            + volume_grad * offsets[k][d]
            for d in range(3)
        ]
        first = [corner[c2][d] - corner[c0][d] for d in range(3)]
        second = [corner[c3][d] - corner[c1][d] for d in range(3)]
        to_first = cross(second, grad)
        to_second = cross(grad, first)
        for d in range(3):
            middle = 0.25 * volume_grad * normals[k][d]
            cots[c0][d] = added(cots[c0][d], middle - 0.5 * to_first[d])
            cots[c2][d] = added(cots[c2][d], middle + 0.5 * to_first[d])
            cots[c1][d] = added(cots[c1][d], middle - 0.5 * to_second[d])
            cots[c3][d] = added(cots[c3][d], middle + 0.5 * to_second[d])
    cots = [[cots[c][d] + center_cot[d] for d in range(3)] for c in range(8)]

    def meet(bit, down, up, at_low, at_high):
        for c in range(8):
            if not c & bit:
                for d in range(3):
                    a, b = cots[c][d], cots[c | bit][d]
                    cots[c][d] = a + jnp.where(at_low, 0.0, down(b))
                    cots[c | bit][d] = b + jnp.where(at_high, 0.0, up(a))

    meet(1, lambda x: pltpu.roll(x, 1, 1), lambda x: pltpu.roll(x, LANES - 1, 1), axial == 0, axial == 3)
    meet(2, lambda x: pltpu.roll(x, 4, 1), lambda x: pltpu.roll(x, LANES - 4, 1), lane < 4, lane >= LANES - 4)
    meet(4, lambda x: pltpu.roll(x, 2, 0), lambda x: pltpu.roll(x, 6, 0), layer == 0, layer == 3)

    sens = [jnp.zeros((8, LANES), jnp.float32) for _ in range(3)]
    for c in range(8):
        for l in range(4):
            chosen = source == c * 4 + l
            for d in range(3):
                got = lanes_at(spread(cots[c][d][2 * l : 2 * l + 1]), within)
                sens[d] = jnp.where(chosen, got, sens[d])

    rs_send[...] = jnp.zeros_like(rs_send)
    for o in range(N_OP):
        for d in range(3):
            rs_send[o, 2 * d : 2 * d + 2, :] = sens[d][2 * o : 2 * o + 2]
    sums = []
    for j, peer in enumerate(peers):
        copy = pltpu.make_async_remote_copy(
            src_ref=rs_send.at[peer],
            dst_ref=rs_recv.at[j],
            send_sem=r_send_sem.at[j],
            recv_sem=r_recv_sem.at[j],
            device_id=(peer, cell),
            device_id_type=MESH,
        )
        copy.start()
        sums.append(copy)

    outbuf[48:56, :] = jnp.zeros((8, CELLS_HERE), jnp.float32)
    for j in range(STATE):
        for l in range(4):
            outbuf[2 * j : 2 * j + 2, l * LANES : (l + 1) * LANES] = adjoint[j][2 * l : 2 * l + 2]
    back = move_cells(outbuf[...], onehot, 0)
    for j in range(STATE):
        out_ref[j] = back[2 * j : 2 * j + 2]
    put = pltpu.make_async_copy(out_ref, out_hbm, out_sem)
    put.start()

    total = rs_send[op]
    for j, copy in enumerate(sums):
        copy.wait()
        total = total + rs_recv[j]
    for d in range(3):
        for h in range(2):
            sens_ref[d : d + 1, h * LANES : (h + 1) * LANES] = total[2 * d + h : 2 * d + h + 1]
    for copy in coord_copies + copies:
        copy.wait_send()
    put.wait()


def per_device(
    flow_state,
    adjoint_start,
    objective_grad,
    adjacency,
    send_list,
    cell_nodes,
    coords,
    jacobians,
    dissipation,
    frequency,
):
    anywhere = pl.BlockSpec(memory_space=pl.ANY)
    f32, i32 = jnp.float32, jnp.int32
    dma = pltpu.SemaphoreType.DMA

    def pairs(x):
        return x.transpose(1, 2, 0, 3).reshape(STATE, OPS_HERE, CELLS_HERE)

    rows = pltpu.VMEM((STATE, OPS_HERE, CELLS_HERE), f32)
    message = pltpu.VMEM((GROUPS, 8, LANES), f32)
    maps = pltpu.VMEM((2, 8, LANES), f32)
    block = pltpu.VMEM((2, STATE, 8, LANES), f32)
    points = pltpu.VMEM((3, 8, 8, LANES), f32)
    packed = pltpu.VMEM((3, 8, 4, LANES), f32)
    adjoint, sens = pl.pallas_call(
        kernel,
        out_shape=(
            jax.ShapeDtypeStruct((STATE, OPS_HERE, CELLS_HERE), f32),
            jax.ShapeDtypeStruct(coords.shape, f32),
        ),
        in_specs=[anywhere] * 10,
        out_specs=(anywhere, pl.BlockSpec(memory_space=pltpu.VMEM)),
        scratch_shapes=[
            rows,
            rows,
            rows,
            pltpu.VMEM((6, CELLS_HERE), i32),
            pltpu.VMEM((2, LANES), i32),
            pltpu.VMEM((8, CELLS_HERE), i32),
            pltpu.VMEM((3, 256), f32),
            pltpu.SMEM((3, VARS, OPS_HERE, VARS), f32),
            pltpu.SMEM((OPS_HERE,), f32),
            pltpu.SMEM((OPS_HERE,), f32),
            rows,
            pltpu.VMEM((N_OP, 3, 256), f32),
            pltpu.VMEM((3, 8, LANES), f32),
            pltpu.VMEM((96, CELLS_HERE), f32),
            pltpu.VMEM((104, CELLS_HERE), f32),
            pltpu.VMEM((3, STATE, 8, LANES), f32),
            pltpu.VMEM((3, 8, 8, LANES), f32),
            pltpu.VMEM((8, 8, LANES), f32),
            message,
            message,
            message,
            message,
            maps,
            maps,
            maps,
            maps,
            block,
            block,
            points,
            points,
            pltpu.VMEM((STATE, 8, LANES), f32),
            packed,
            packed,
            packed,
            pltpu.VMEM((N_OP, 8, LANES), f32),
            pltpu.VMEM((N_OP - 1, 8, LANES), f32),
            pltpu.VMEM((56, CELLS_HERE), f32),
            dma((10,)),
            dma,
            dma((3,)),
            dma((3,)),
            dma((3,)),
            dma((3,)),
            dma((5,)),
            dma((5,)),
            dma((5,)),
            dma((5,)),
        ],
        compiler_params=pltpu.CompilerParams(collective_id=0, has_side_effects=True),
    )(
        pairs(flow_state),
        pairs(adjoint_start),
        pairs(objective_grad),
        adjacency,
        send_list.reshape(2, LANES),
        cell_nodes,
        coords,
        jacobians.transpose(1, 2, 0, 3),
        dissipation,
        frequency,
    )
    adjoint = adjoint.reshape(INST, VARS, OPS_HERE, CELLS_HERE).transpose(2, 0, 1, 3)
    return adjoint, sens


def solution(mesh):
    in_specs = (
        P("op", None, None, "cell"),
        P("op", None, None, "cell"),
        P("op", None, None, "cell"),
        P(None, "cell"),
        P("cell"),
        P(None, "cell"),
        P(None, ("op", "cell")),
        P("op", None, None, None),
        P("op"),
        P("op"),
    )
    out_specs = (P("op", None, None, "cell"), P(None, ("op", "cell")))
    return jax.shard_map(
        per_device, mesh=mesh, in_specs=in_specs, out_specs=out_specs, check_vma=False
    )
```
